512 devices in a mesh: gen: 32 (over x_hi, z), tm: 16 (over x_lo, y, core).
Axes of the slice: x: 4 (x_hi: 2, x_lo: 2; x = x_hi * 2 + x_lo), y: 4, z: 16, core: 2. Of those that a mesh axis runs over, the one named last changes fastest.
Arguments:
- relation: bfloat16 [25600, 25600], P('gen', 'tm'), may hold values from -1 to 3
- effects: float32 [25600, 1024], P('tm', 'gen'), may hold values from -6 to 6
- phi_one: float32 [1024], replicated, may hold values from 0.3 to 1.2
- phi_two: float32 [1024], replicated, may hold values from -0.7 to 0.3
- innov_scale: float32 [1024], replicated, may hold values from 0.4 to 2.5
Outputs:
- applied: float32 [25600, 1024], P('gen', 'tm')
The draws below stay inside these ranges and needn't reach their ends.
All inputs are finite; a program needn't handle non-finite values.
Results may differ from the reference program's by a relative error of at most 0.0003.
Values sent between devices are 32-bit elements; how exact they have to be, the bound alone decides.
A program may use at most 64 MiB of HBM per device.

```python
import math
import jax
import jax.numpy as jnp
from jax import lax

ANI_DEV = 800
TIMES = 1024
ANIMALS = 25600
N_GEN = 32


def draw_relation(key, part):
    key_off, key_diag = jax.random.split(jax.random.fold_in(key, 11))
    spread = ANIMALS ** (-0.5)
    raw = jnp.clip(jax.random.normal(key_off, (ANIMALS, ANIMALS), jnp.float32), -6.0, 6.0)
    indices = jnp.arange(ANIMALS, dtype=jnp.int32)
    upper = indices[:, None] < indices[None, :]
    offdiag = jnp.where(upper, raw, raw.T) * spread
    diagonal = jax.random.uniform(key_diag, (ANIMALS,), jnp.float32, 1.5, 2.5)
    on_diag = indices[:, None] == indices[None, :]
    return jnp.where(on_diag, diagonal[None, :], offdiag).astype(jnp.bfloat16)


def block_scale(stream_key, dims, shards, smallest, high):
    def one(dim, shards_of):
        steps = jax.random.uniform(jax.random.fold_in(jax.random.fold_in(stream_key, 6), dim), (shards_of,), jnp.float32, smallest / len(shards), high / len(shards))
        return jnp.repeat(jnp.exp(steps), dims[dim] // shards_of).reshape((-1,) + (1,) * (len(dims) - dim - 1))

    gain = one(*shards[0])
    for cut in shards[1:]:
        gain = gain * one(*cut)
    return gain


def normal_values(key, dims, width, most, shards=(), kind=jnp.bfloat16):
    values = jax.random.normal(key, dims, jnp.float32) * width
    if len(shards) > 0:
        values = block_scale(key, dims, shards, -0.22, 0.18) * values
    return jnp.clip(values, min=-most, max=most).astype(kind)


def setup_inputs(seed: int = 0) -> dict:
    keys = jax.random.split(jax.random.key(seed), 6)
    relation = draw_relation(jax.random.fold_in(keys[5], 71), 0)
    effects = normal_values(keys[1], (ANIMALS, TIMES), 1.0, 6.0, ((0, 16), (1, 32)), jnp.float32)
    phi_one = jnp.clip(jax.random.uniform(keys[2], (TIMES,), jnp.float32, 0.3, 1.2), 0.3, 1.2)
    phi_two = jnp.clip(jax.random.uniform(keys[3], (TIMES,), jnp.float32, -0.7, 0.3), -0.7, 0.3)
    innov_scale = jnp.clip(jnp.exp(jax.random.uniform(keys[4], (TIMES,), jnp.float32, math.log(0.4), math.log(2.5))), 0.4, 2.5)
    return dict(relation=relation, effects=effects, phi_one=phi_one, phi_two=phi_two, innov_scale=innov_scale)


def temporal_apply(field, phi_one, phi_two, innov_scale):
    zero_pair = jnp.zeros((2,), jnp.float32)
    first_pad = jnp.concatenate([phi_one, zero_pair])
    second_pad = jnp.concatenate([phi_two, zero_pair])
    scale_pad = jnp.concatenate([innov_scale, zero_pair])
    widened = jnp.pad(field, ((0, 0), (2, 2)))
    innov = widened[:, 2:] - first_pad[None, :] * widened[:, 1:-1] - second_pad[None, :] * widened[:, :-2]
    weighted = scale_pad[None, :] * innov
    count = field.shape[1]
    return (weighted[:, :count]
            - first_pad[None, 1:count + 1] * weighted[:, 1:count + 1]
            - second_pad[None, 2:count + 2] * weighted[:, 2:count + 2])


def reference(relation, effects, phi_one, phi_two, innov_scale):
    row_blocks = relation.reshape(N_GEN, ANI_DEV, ANIMALS)

    def block_rows(rows):
        return jnp.dot(rows.astype(jnp.float32), effects, precision=lax.Precision.HIGHEST,
                       preferred_element_type=jnp.float32)

    genetic = lax.map(block_rows, row_blocks).reshape(ANIMALS, TIMES)
    return temporal_apply(genetic, phi_one, phi_two, innov_scale)
```

```python
import jax
import jax.numpy as jnp
from jax import lax
from jax.experimental import pallas as pl
from jax.experimental.pallas import tpu as pltpu
from jax.sharding import PartitionSpec as P

MESH = pl.DeviceIdType.MESH
NZ = 16
ANI = 800
COLS = 1600
TB = 32
FULL = COLS // 128
REST = COLS - 128 * FULL
HALF = 200
CUTS = ((0, 200), (200, 48), (248, 152))


def kernel(
    rel_hbm, eff_hbm, phi_one, phi_two, scale, out_ref,
    rel, xe, wb, cf, hsend, hrecv, gx, lhs, part, r1, r2, r3,
    lsem, hss, hrs, zss, zrs, xss, xrs, s1s, s1r, s2s, s2r, s3s, s3r,
):
    g = lax.axis_index("gen")
    t = lax.axis_index("tm")
    h, z = g // NZ, g % NZ
    x_lo, y, c = t // 8, (t // 2) % 4, t % 2

    up = (h * NZ + (z + 1) % NZ, t)
    down = (h * NZ + (z + NZ - 1) % NZ, t)
    after = ((g + 1) % 32, t)
    before = ((g + 31) % 32, t)
    far = ((1 - h) * NZ + z, t)
    core = (g, t + 1 - 2 * c)
    side = (g, (1 - x_lo) * 8 + y * 2 + c)

    def at_y(yy):
        return (g, x_lo * 8 + yy * 2 + c)

    load_rel = pltpu.make_async_copy(rel_hbm, rel, lsem.at[0])
    load_eff = pltpu.make_async_copy(eff_hbm, xe.at[pl.ds(8, TB)], lsem.at[1])
    load_eff.start()
    load_rel.start()

    barrier = pltpu.get_barrier_semaphore()
    peers = [up, down, after, before, far, core, side] + [
        at_y((y + d) % 4) for d in (1, 2, 3)
    ]
    for peer in peers:
        pl.semaphore_signal(barrier, inc=1, device_id=peer, device_id_type=MESH)

    first = g * TB
    for i in range(TB + 2):
        where = jnp.minimum(first + i, 1023)
        inside = first + i < 1024
        for row, coef in enumerate((phi_one, phi_two, scale)):
            value = jnp.where(inside, coef[where], 0.0)
            cf[row, pl.ds(8 + i, 1), :] = jnp.full((1, 128), value, jnp.float32)

    load_eff.wait()
    for k in range(FULL + 1):
        width = 128 if k < FULL else REST
        lanes = pl.ds(128 * k, width)
        for r in range(2):
            hsend[0, pl.ds(16 * r + k, 1), pl.ds(0, width)] = xe[pl.ds(38 + r, 1), lanes]
            hsend[1, pl.ds(16 * r + k, 1), pl.ds(0, width)] = xe[pl.ds(8 + r, 1), lanes]

    pl.semaphore_wait(barrier, len(peers))

    def halo(i, to):
        return pltpu.make_async_remote_copy(
            src_ref=hsend.at[i], dst_ref=hrecv.at[i], send_sem=hss.at[i],
            recv_sem=hrs.at[i], device_id=to, device_id_type=MESH,
        )

    halo(0, after).start()
    halo(1, before).start()

    def zcopy(stream, step, piece, zp):
        col = 0 if piece < 3 else 1
        rows = pl.ds(*CUTS[min(piece, 2)])
        place = gx.at[col, zp, rows]
        return pltpu.make_async_remote_copy(
            src_ref=place, dst_ref=place, send_sem=zss.at[stream, step, piece],
            recv_sem=zrs.at[stream, step, piece],
            device_id=up if stream == 0 else down, device_id_type=MESH,
        )

    def xcopy(zp, piece):
        rows = pl.ds(*CUTS[piece])
        return pltpu.make_async_remote_copy(
            src_ref=gx.at[0, zp, rows], dst_ref=gx.at[1, zp, rows],
            send_sem=xss.at[zp, piece], recv_sem=xrs.at[zp, piece],
            device_id=far, device_id_type=MESH,
        )

    def coef(i, start, rows, width):
        return cf[i, pl.ds(start, rows), pl.ds(0, width)]

    def weigh(start, rows, lanes, width):
        innov = (
            xe[pl.ds(start, rows), lanes]
            - coef(0, start, rows, width) * xe[pl.ds(start - 1, rows), lanes]
            - coef(1, start, rows, width) * xe[pl.ds(start - 2, rows), lanes]
        )
        wb[pl.ds(start, rows), lanes] = coef(2, start, rows, width) * innov

    def lag(start, rows, lanes, width):
        return (
            wb[pl.ds(start, rows), lanes]
            - coef(0, start + 1, rows, width) * wb[pl.ds(start + 1, rows), lanes]
            - coef(1, start + 2, rows, width) * wb[pl.ds(start + 2, rows), lanes]
        )

    for k in range(FULL + 1):
        width = 128 if k < FULL else REST
        lanes = pl.ds(128 * k, width)
        weigh(8, TB, lanes, width)
        mid = lag(16, 16, lanes, width)
        if k < FULL:
            gx[0, z, pl.ds(16 * k, 16), :] = mid
        else:
            gx[0, z, pl.ds(16 * k, 8), :] = jnp.concatenate([mid[:8], mid[8:]], axis=1)

    xcopy(z, 0).start()
    zcopy(0, 1, 0, z).start()
    zcopy(1, 1, 0, z).start()

    halo(0, after).wait_recv()
    halo(1, before).wait_recv()
    for k in range(FULL + 1):
        width = 128 if k < FULL else REST
        lanes = pl.ds(128 * k, width)
        for r in range(2):
            old = hrecv[0, pl.ds(16 * r + k, 1), pl.ds(0, width)]
            new = hrecv[1, pl.ds(16 * r + k, 1), pl.ds(0, width)]
            xe[pl.ds(6 + r, 1), lanes] = jnp.where(g > 0, old, 0.0)
            xe[pl.ds(40 + r, 1), lanes] = jnp.where(g < 31, new, 0.0)
    for k in range(FULL + 1):
        width = 128 if k < FULL else REST
        lanes = pl.ds(128 * k, width)
        weigh(8, 8, lanes, width)
        weigh(40, 2, lanes, width)
        head = lag(8, 8, lanes, width)
        tail = lag(32, 8, lanes, width)
        if k < FULL:
            gx[0, z, pl.ds(HALF + 16 * k, 8), :] = head
            gx[0, z, pl.ds(HALF + 16 * k + 8, 8), :] = tail
        else:
            gx[0, z, pl.ds(HALF + 16 * k, 8), :] = jnp.concatenate([head, tail], axis=1)

    xcopy(z, 2).start()
    xcopy(z, 1).start()
    for piece in (1, 2):
        zcopy(0, 1, piece, z).start()
        zcopy(1, 1, piece, z).start()
    xcopy(z, 2).wait_recv()
    zcopy(0, 1, 3, z).start()
    zcopy(1, 1, 3, z).start()
    load_rel.wait()

    def place_of(i):
        q = i // 2
        return jnp.where(i % 2 == 0, (z + q) % NZ, (z + NZ - q) % NZ)

    def core_of(zp):
        return (zp // 2) % 2

    def core_copy(zp):
        return pltpu.make_async_remote_copy(
            src_ref=part.at[zp], dst_ref=r1.at[zp], send_sem=s1s.at[zp],
            recv_sem=s1r.at[zp], device_id=core, device_id_type=MESH,
        )

    def y_copy(zp, yy, slot):
        return pltpu.make_async_remote_copy(
            src_ref=part.at[zp], dst_ref=r2.at[zp % 2, slot], send_sem=s2s.at[zp],
            recv_sem=s2r.at[zp % 2, slot], device_id=at_y(yy), device_id_type=MESH,
        )

    mine = (h + x_lo) % 2

    def side_copy(zp):
        return pltpu.make_async_remote_copy(
            src_ref=part.at[zp, 1 - mine], dst_ref=r3.at[zp % 2],
            send_sem=s3s.at[zp % 2], recv_sem=s3r.at[zp % 2],
            device_id=side, device_id_type=MESH,
        )

    def split(block, at, lanes):
        high = block.astype(jnp.bfloat16)
        low = (block - high.astype(jnp.float32)).astype(jnp.bfloat16)
        lhs[pl.ds(at, 16), lanes] = high
        lhs[pl.ds(64 + at, 16), lanes] = low

    def multiply(zp):
        for col in range(2):
            for half in range(2):
                at = col * TB + half * 16
                base = half * HALF
                for k in range(FULL):
                    split(gx[col, zp, pl.ds(base + 16 * k, 16), :], at, pl.ds(128 * k, 128))
                rest = gx[col, zp, pl.ds(base + 16 * FULL, 8), :]
                rest = jnp.concatenate([rest[:, :REST], rest[:, REST:]], axis=0)
                split(rest, at, pl.ds(128 * FULL, REST))
        both = lax.dot_general(
            lhs[...], rel[...], (((1,), (1,)), ((), ())),
            preferred_element_type=jnp.float32,
        )
        total = both[:64] + both[64:]
        part[zp, 0] = total[:TB]
        part[zp, 1] = total[TB:]

    def body(i, carry):
        s = (i + 1) // 2
        zu, zd = (z + NZ - s) % NZ, (z + s) % NZ

        @pl.when((i % 2 == 1) & (i <= 16))
        def _():
            for piece in (0, 1):
                zcopy(0, s, piece, zu).wait_recv()

                @pl.when(s < 8)
                def _():
                    zcopy(0, s + 1, piece, zu).start()

                xcopy(zu, piece).start()

                @pl.when(s < 8)
                def _():
                    zcopy(1, s, piece, zd).wait_recv()

                    @pl.when(s < 7)
                    def _():
                        zcopy(1, s + 1, piece, zd).start()

                    xcopy(zd, piece).start()

        @pl.when((i % 2 == 0) & (i <= 16))
        def _():
            for piece in (2, 3):
                zcopy(1, s, piece, zd).wait_recv()

                @pl.when(s < 8)
                def _():
                    zcopy(1, s + 1, piece, zd).start()
                    zcopy(0, s, piece, zu).wait_recv()

                    @pl.when(s < 7)
                    def _():
                        zcopy(0, s + 1, piece, zu).start()

        @pl.when(i <= 16)
        def _():
            zp = place_of(i)
            xcopy(zp, 0).wait_recv()
            xcopy(zp, 1).wait_recv()
            multiply(zp)

            @pl.when(core_of(zp) != c)
            def _():
                core_copy(zp).start()

        @pl.when((i >= 2) & (i <= 17))
        def _():
            zp = place_of(i - 1)

            @pl.when(core_of(zp) == c)
            def _():
                core_copy(zp).wait_recv()
                part[zp] = part[zp] + r1[zp]
                yy = zp // 4

                @pl.when(yy != y)
                def _():
                    y_copy(zp, yy, (y + 3 - yy) % 4).start()

        @pl.when(i >= 3)
        def _():
            zp = place_of(i - 2)

            @pl.when((core_of(zp) == c) & (zp // 4 == y))
            def _():
                for slot in range(3):
                    y_copy(zp, y, slot).wait_recv()
                part[zp] = part[zp] + (r2[zp % 2, 0] + (r2[zp % 2, 1] + r2[zp % 2, 2]))
                side_copy(zp).start()

        return carry

    lax.fori_loop(1, 19, body, 0)

    for b in range(2):
        zp = 4 * y + 2 * c + b
        side_copy(zp).wait_recv()
        total = part[zp, mine] + r3[b]
        out_ref[pl.ds(b * TB + 8, 16), :] = total[:16]
        out_ref[pl.ds(b * TB, 8), :] = total[16:24]
        out_ref[pl.ds(b * TB + 24, 8), :] = total[24:]

    halo(0, after).wait_send()
    halo(1, before).wait_send()

    def drain(s, carry):
        for stream in range(2):
            for piece in range(4):

                @pl.when((s < 8) | ((piece < 2) == (stream == 0)))
                def _():
                    zcopy(stream, s, piece, z).wait_send()

        return carry

    lax.fori_loop(1, 9, drain, 0)

    def drain_z(zp, carry):
        xcopy(zp, 0).wait_send()
        xcopy(zp, 1).wait_send()

        @pl.when(core_of(zp) != c)
        def _():
            core_copy(zp).wait_send()

        @pl.when((core_of(zp) == c) & (zp // 4 != y))
        def _():
            y_copy(zp, y, 0).wait_send()

        return carry

    lax.fori_loop(0, NZ, drain_z, 0)
    xcopy(z, 2).wait_send()
    for b in range(2):
        side_copy(4 * y + 2 * c + b).wait_send()


def on_device(relation, effects, phi_one, phi_two, innov_scale):
    dma = pltpu.SemaphoreType.DMA
    f32 = jnp.float32
    applied = pl.pallas_call(
        kernel,
        out_shape=jax.ShapeDtypeStruct((2 * TB, ANI), f32),
        in_specs=[pl.BlockSpec(memory_space=pl.ANY)] * 2
        + [pl.BlockSpec(memory_space=pltpu.SMEM)] * 3,
        out_specs=pl.BlockSpec(memory_space=pltpu.VMEM),
        scratch_shapes=[
            pltpu.VMEM((ANI, COLS), jnp.bfloat16),
            pltpu.VMEM((48, COLS), f32),
            pltpu.VMEM((48, COLS), f32),
            pltpu.VMEM((3, 48, 128), f32),
            pltpu.VMEM((2, 32, 128), f32),
            pltpu.VMEM((2, 32, 128), f32),
            pltpu.VMEM((2, NZ, 2 * HALF, 128), f32),
            pltpu.VMEM((128, COLS), jnp.bfloat16),
            pltpu.VMEM((NZ, 2, TB, ANI), f32),
            pltpu.VMEM((NZ, 2, TB, ANI), f32),
            pltpu.VMEM((2, 3, 2, TB, ANI), f32),
            pltpu.VMEM((2, TB, ANI), f32),
            dma((2,)), dma((2,)), dma((2,)),
            dma((2, 9, 4)), dma((2, 9, 4)), dma((NZ, 3)), dma((NZ, 3)),
            dma((NZ,)), dma((NZ,)), dma((NZ,)), dma((2, 3)), dma((2,)), dma((2,)),
        ],
        compiler_params=pltpu.CompilerParams(
            collective_id=0, has_side_effects=True, vmem_limit_bytes=56 << 20
        ),
    )(relation, effects.T, phi_one, phi_two, innov_scale)
    return applied.T


def solution(mesh):
    placed = (P("gen", "tm"), P("tm", "gen"), P(), P(), P())
    return jax.shard_map(
        on_device, mesh=mesh, in_specs=placed, out_specs=P("gen", "tm"), check_vma=False
    )
```

```python
import jax
import jax.numpy as jnp
from jax import lax
from jax.experimental import pallas as pl
from jax.experimental.pallas import tpu as pltpu
from jax.sharding import PartitionSpec as P

MESH = pl.DeviceIdType.MESH
NZ = 16
ANI = 800
COLS = 1600
TB = 32
FULL = COLS // 128
REST = COLS - 128 * FULL
HALF = 200
LAG_X, LAG_CORE, LAG_Y, LAG_SIDE = 2, 3, 5, 7
CUTS = ((0, 200), (200, 48), (248, 152))


def kernel(
    rel_hbm, eff_hbm, one_hbm, two_hbm, scale_hbm, out_ref,
    rel, xe, wb, cf, hsend, hrecv, gx, lhs, part, r1, r2, r3, done, phi_one, phi_two, scale,
    lsem, hss, hrs, zss, zrs, xss, xrs, s1s, s1r, s2s, s2r, s3s, s3r, s4s, s4r,
):
    g = lax.axis_index("gen")
    t = lax.axis_index("tm")
    h, z = g // NZ, g % NZ
    x_lo, y, c = t // 8, (t // 2) % 4, t % 2

    up = (h * NZ + (z + 1) % NZ, t)
    down = (h * NZ + (z + NZ - 1) % NZ, t)
    after = ((g + 1) % 32, t)
    before = ((g + 31) % 32, t)
    far = ((1 - h) * NZ + z, t)
    core = (g, t + 1 - 2 * c)
    side = (g, (1 - x_lo) * 8 + y * 2 + c)

    def at_y(yy):
        return (g, x_lo * 8 + yy * 2 + c)

    load_rel = pltpu.make_async_copy(rel_hbm, rel, lsem.at[0])
    load_eff = pltpu.make_async_copy(eff_hbm, xe.at[pl.ds(8, TB)], lsem.at[1])
    load_coefs = [
        pltpu.make_async_copy(src, dst, lsem.at[2 + i])
        for i, (src, dst) in enumerate(
            ((one_hbm, phi_one), (two_hbm, phi_two), (scale_hbm, scale))
        )
    ]
    load_eff.start()
    for load in load_coefs:
        load.start()
    load_rel.start()

    barrier = pltpu.get_barrier_semaphore()
    peers = [up, down, after, before, far, core, side] + [
        at_y((y + d) % 4) for d in (1, 2, 3)
    ]
    for peer in peers:
        pl.semaphore_signal(barrier, inc=1, device_id=peer, device_id_type=MESH)

    for load in load_coefs:
        load.wait()
    first = g * TB
    for i in range(TB + 2):
        where = jnp.minimum(first + i, 1023)
        inside = first + i < 1024
        for row, coef in enumerate((phi_one, phi_two, scale)):
            value = jnp.where(inside, coef[where], 0.0)
            cf[row, pl.ds(8 + i, 1), :] = jnp.full((1, 128), value, jnp.float32)

    load_eff.wait()
    for k in range(FULL + 1):
        width = 128 if k < FULL else REST
        lanes = pl.ds(128 * k, width)
        for r in range(2):
            hsend[0, pl.ds(16 * r + k, 1), pl.ds(0, width)] = xe[pl.ds(38 + r, 1), lanes]
            hsend[1, pl.ds(16 * r + k, 1), pl.ds(0, width)] = xe[pl.ds(8 + r, 1), lanes]

    pl.semaphore_wait(barrier, len(peers))

    def halo(i, to):
        return pltpu.make_async_remote_copy(
            src_ref=hsend.at[i], dst_ref=hrecv.at[i], send_sem=hss.at[i],
            recv_sem=hrs.at[i], device_id=to, device_id_type=MESH,
        )

    halo(0, after).start()
    halo(1, before).start()

    def zcopy(stream, step, piece, zp):
        col = 0 if piece < 3 else 1
        rows = pl.ds(*CUTS[min(piece, 2)])
        place = gx.at[col, zp, rows]
        return pltpu.make_async_remote_copy(
            src_ref=place, dst_ref=place, send_sem=zss.at[stream, step, piece],
            recv_sem=zrs.at[stream, step, piece],
            device_id=up if stream == 0 else down, device_id_type=MESH,
        )

    def xcopy(zp, piece):
        rows = pl.ds(*CUTS[piece])
        return pltpu.make_async_remote_copy(
            src_ref=gx.at[0, zp, rows], dst_ref=gx.at[1, zp, rows],
            send_sem=xss.at[zp, piece], recv_sem=xrs.at[zp, piece],
            device_id=far, device_id_type=MESH,
        )

    def coef(i, start, rows, width):
        return cf[i, pl.ds(start, rows), pl.ds(0, width)]

    def weigh(start, rows, lanes, width):
        innov = (
            xe[pl.ds(start, rows), lanes]
            - coef(0, start, rows, width) * xe[pl.ds(start - 1, rows), lanes]
            - coef(1, start, rows, width) * xe[pl.ds(start - 2, rows), lanes]
        )
        wb[pl.ds(start, rows), lanes] = coef(2, start, rows, width) * innov

    def lag(start, rows, lanes, width):
        return (
            wb[pl.ds(start, rows), lanes]
            - coef(0, start + 1, rows, width) * wb[pl.ds(start + 1, rows), lanes]
            - coef(1, start + 2, rows, width) * wb[pl.ds(start + 2, rows), lanes]
        )

    for k in range(FULL + 1):
        width = 128 if k < FULL else REST
        lanes = pl.ds(128 * k, width)
        weigh(8, TB, lanes, width)
        mid = lag(16, 16, lanes, width)
        if k < FULL:
            gx[0, z, pl.ds(16 * k, 16), :] = mid
        else:
            gx[0, z, pl.ds(16 * k, 8), :] = jnp.concatenate([mid[:8], mid[8:]], axis=1)

    xcopy(z, 0).start()
    zcopy(0, 1, 0, z).start()
    zcopy(1, 1, 0, z).start()

    halo(0, after).wait_recv()
    halo(1, before).wait_recv()
    for k in range(FULL + 1):
        width = 128 if k < FULL else REST
        lanes = pl.ds(128 * k, width)
        for r in range(2):
            old = hrecv[0, pl.ds(16 * r + k, 1), pl.ds(0, width)]
            new = hrecv[1, pl.ds(16 * r + k, 1), pl.ds(0, width)]
            xe[pl.ds(6 + r, 1), lanes] = jnp.where(g > 0, old, 0.0)
            xe[pl.ds(40 + r, 1), lanes] = jnp.where(g < 31, new, 0.0)
    for k in range(FULL + 1):
        width = 128 if k < FULL else REST
        lanes = pl.ds(128 * k, width)
        weigh(8, 8, lanes, width)
        weigh(40, 2, lanes, width)
        head = lag(8, 8, lanes, width)
        tail = lag(32, 8, lanes, width)
        if k < FULL:
            gx[0, z, pl.ds(HALF + 16 * k, 8), :] = head
            gx[0, z, pl.ds(HALF + 16 * k + 8, 8), :] = tail
        else:
            gx[0, z, pl.ds(HALF + 16 * k, 8), :] = jnp.concatenate([head, tail], axis=1)

    xcopy(z, 2).start()
    xcopy(z, 1).start()
    for piece in (1, 2):
        zcopy(0, 1, piece, z).start()
        zcopy(1, 1, piece, z).start()
    xcopy(z, 2).wait_recv()
    zcopy(0, 1, 3, z).start()
    zcopy(1, 1, 3, z).start()
    load_rel.wait()

    def place_of(i):
        q = i // 2
        return jnp.where(i % 2 == 0, (z + q) % NZ, (z + NZ - q) % NZ)

    def core_of(zp):
        return (zp // 2) % 2

    def core_copy(zp):
        return pltpu.make_async_remote_copy(
            src_ref=part.at[zp], dst_ref=r1.at[zp], send_sem=s1s.at[zp],
            recv_sem=s1r.at[zp], device_id=core, device_id_type=MESH,
        )

    def y_copy(zp, d):
        q = (y + d) % 4
        return pltpu.make_async_remote_copy(
            src_ref=part.at[zp, :, pl.ds(pl.multiple_of(8 * q, 8), 8)],
            dst_ref=r2.at[zp, d - 1], send_sem=s2s.at[zp, d - 1],
            recv_sem=s2r.at[zp, d - 1], device_id=at_y(q), device_id_type=MESH,
        )

    mine = (h + x_lo) % 2
    quarter = pl.ds(pl.multiple_of(8 * y, 8), 8)

    def side_copy(zp):
        return pltpu.make_async_remote_copy(
            src_ref=part.at[zp, 1 - mine, quarter], dst_ref=r3.at[zp],
            send_sem=s3s.at[zp], recv_sem=s3r.at[zp],
            device_id=side, device_id_type=MESH,
        )

    def home_copy(zp, q):
        return pltpu.make_async_remote_copy(
            src_ref=part.at[zp, mine, quarter], dst_ref=done.at[zp % 2, q],
            send_sem=s4s.at[zp], recv_sem=s4r.at[zp % 2, q],
            device_id=at_y(zp // 4), device_id_type=MESH,
        )

    def split(block, at, lanes):
        high = block.astype(jnp.bfloat16)
        low = (block - high.astype(jnp.float32)).astype(jnp.bfloat16)
        lhs[pl.ds(at, 16), lanes] = high
        lhs[pl.ds(64 + at, 16), lanes] = low

    def multiply(zp):
        for col in range(2):
            for half in range(2):
                at = col * TB + half * 16
                base = half * HALF
                for k in range(FULL):
                    split(gx[col, zp, pl.ds(base + 16 * k, 16), :], at, pl.ds(128 * k, 128))
                rest = gx[col, zp, pl.ds(base + 16 * FULL, 8), :]
                rest = jnp.concatenate([rest[:, :REST], rest[:, REST:]], axis=0)
                split(rest, at, pl.ds(128 * FULL, REST))
        both = lax.dot_general(
            lhs[...], rel[...], (((1,), (1,)), ((), ())),
            preferred_element_type=jnp.float32,
        )
        total = both[:64] + both[64:]
        part[zp, 0] = total[:TB]
        part[zp, 1] = total[TB:]

    def body(i, carry):
        s = (i + 1) // 2
        zu, zd = (z + NZ - s) % NZ, (z + s) % NZ

        @pl.when((i % 2 == 1) & (i <= 16))
        def _():
            for piece in (0, 1):
                zcopy(0, s, piece, zu).wait_recv()

                @pl.when(s < 8)
                def _():
                    zcopy(0, s + 1, piece, zu).start()

                xcopy(zu, piece).start()

                @pl.when(s < 8)
                def _():
                    zcopy(1, s, piece, zd).wait_recv()

                    @pl.when(s < 7)
                    def _():
                        zcopy(1, s + 1, piece, zd).start()

                    xcopy(zd, piece).start()

        @pl.when((i % 2 == 0) & (i <= 16))
        def _():
            for piece in (2, 3):
                zcopy(1, s, piece, zd).wait_recv()

                @pl.when(s < 8)
                def _():
                    zcopy(1, s + 1, piece, zd).start()
                    zcopy(0, s, piece, zu).wait_recv()

                    @pl.when(s < 7)
                    def _():
                        zcopy(0, s + 1, piece, zu).start()

        @pl.when((i > LAG_X) & (i <= 16 + LAG_X))
        def _():
            zp = place_of(i - LAG_X)
            xcopy(zp, 0).wait_recv()
            xcopy(zp, 1).wait_recv()
            multiply(zp)

            @pl.when(core_of(zp) != c)
            def _():
                core_copy(zp).start()

        @pl.when((i > LAG_CORE) & (i <= 16 + LAG_CORE))
        def _():
            zp = place_of(i - LAG_CORE)

            @pl.when(core_of(zp) == c)
            def _():
                core_copy(zp).wait_recv()
                part[zp] = part[zp] + r1[zp]
                for d in (1, 2, 3):
                    y_copy(zp, d).start()

        @pl.when((i > LAG_Y) & (i <= 16 + LAG_Y))
        def _():
            zp = place_of(i - LAG_Y)

            @pl.when(core_of(zp) == c)
            def _():
                for d in (1, 2, 3):
                    y_copy(zp, d).wait_recv()
                both = r2[zp, 0] + (r2[zp, 1] + r2[zp, 2])
                part[zp, :, quarter] = part[zp, :, quarter] + both
                side_copy(zp).start()

        @pl.when(i > LAG_SIDE)
        def _():
            zp = place_of(i - LAG_SIDE)

            @pl.when(core_of(zp) == c)
            def _():
                side_copy(zp).wait_recv()
                total = part[zp, mine, quarter] + r3[zp]
                part[zp, mine, quarter] = total

                @pl.when(zp // 4 == y)
                def _():
                    done[zp % 2, y] = total

                @pl.when(zp // 4 != y)
                def _():
                    home_copy(zp, y).start()

        return carry

    lax.fori_loop(1, 17 + LAG_SIDE, body, 0)

    for d in (1, 2, 3):
        for b in range(2):
            home_copy(4 * y + 2 * c + b, (y + d) % 4).wait_recv()
    for b in range(2):
        for q, row in enumerate((8, 16, 0, 24)):
            out_ref[pl.ds(b * TB + row, 8), :] = done[b, q]

    halo(0, after).wait_send()
    halo(1, before).wait_send()

    def drain(s, carry):
        for stream in range(2):
            for piece in range(4):

                @pl.when((s < 8) | ((piece < 2) == (stream == 0)))
                def _():
                    zcopy(stream, s, piece, z).wait_send()

        return carry

    lax.fori_loop(1, 9, drain, 0)

    def drain_z(zp, carry):
        xcopy(zp, 0).wait_send()
        xcopy(zp, 1).wait_send()

        @pl.when(core_of(zp) != c)
        def _():
            core_copy(zp).wait_send()

        @pl.when(core_of(zp) == c)
        def _():
            for d in (1, 2, 3):
                y_copy(zp, d).wait_send()
            side_copy(zp).wait_send()

            @pl.when(zp // 4 != y)
            def _():
                home_copy(zp, y).wait_send()

        return carry

    lax.fori_loop(0, NZ, drain_z, 0)
    xcopy(z, 2).wait_send()


def on_device(relation, effects, phi_one, phi_two, innov_scale):
    dma = pltpu.SemaphoreType.DMA
    f32 = jnp.float32
    applied = pl.pallas_call(
        kernel,
        out_shape=jax.ShapeDtypeStruct((2 * TB, ANI), f32),
        in_specs=[pl.BlockSpec(memory_space=pl.ANY)] * 5,
        out_specs=pl.BlockSpec(memory_space=pltpu.VMEM),
        scratch_shapes=[
            pltpu.VMEM((ANI, COLS), jnp.bfloat16),
            pltpu.VMEM((48, COLS), f32),
            pltpu.VMEM((48, COLS), f32),
            pltpu.VMEM((3, 48, 128), f32),
            pltpu.VMEM((2, 32, 128), f32),
            pltpu.VMEM((2, 32, 128), f32),
            pltpu.VMEM((2, NZ, 2 * HALF, 128), f32),
            pltpu.VMEM((128, COLS), jnp.bfloat16),
            pltpu.VMEM((NZ, 2, TB, ANI), f32),
            pltpu.VMEM((NZ, 2, TB, ANI), f32),
            pltpu.VMEM((NZ, 3, 2, 8, ANI), f32),
            pltpu.VMEM((NZ, 8, ANI), f32),
            pltpu.VMEM((2, 4, 8, ANI), f32),
            pltpu.SMEM((1024,), f32),
            pltpu.SMEM((1024,), f32),
            pltpu.SMEM((1024,), f32),
            dma((5,)), dma((2,)), dma((2,)),
            dma((2, 9, 4)), dma((2, 9, 4)), dma((NZ, 3)), dma((NZ, 3)),
            dma((NZ,)), dma((NZ,)), dma((NZ, 3)), dma((NZ, 3)), dma((NZ,)), dma((NZ,)),
            dma((NZ,)), dma((2, 4)),
        ],
        compiler_params=pltpu.CompilerParams(
            collective_id=0, has_side_effects=True, vmem_limit_bytes=56 << 20
        ),
    )(relation, effects.T, phi_one, phi_two, innov_scale)
    return applied.T


def solution(mesh):
    placed = (P("gen", "tm"), P("tm", "gen"), P(), P(), P())
    return jax.shard_map(
        on_device, mesh=mesh, in_specs=placed, out_specs=P("gen", "tm"), check_vma=False
    )
```

```python
import jax
import jax.numpy as jnp
from jax import lax
from jax.experimental import pallas as pl
from jax.experimental.pallas import tpu as pltpu
from jax.sharding import PartitionSpec as P

MESH = pl.DeviceIdType.MESH
NZ = 16
ANI = 800
COLS = 1600
TB = 32
FULL = COLS // 128
REST = COLS - 128 * FULL
HALF = 200
LAG_X, LAG_CORE, LAG_Y, LAG_SIDE = 2, 3, 6, 9
CUTS = ((0, 200), (200, 48), (248, 152))


def kernel(
    rel_hbm, eff_hbm, one_hbm, two_hbm, scale_hbm, out_ref,
    rel, xe, wb, cf, hsend, hrecv, gx, lhs, part, r1, r2, r3, done, phi_one, phi_two, scale,
    lsem, hss, hrs, zss, zrs, xss, xrs, s1s, s1r, s2s, s2r, s3s, s3r, s4s, s4r,
):
    g = lax.axis_index("gen")
    t = lax.axis_index("tm")
    h, z = g // NZ, g % NZ
    x_lo, y, c = t // 8, (t // 2) % 4, t % 2

    up = (h * NZ + (z + 1) % NZ, t)
    down = (h * NZ + (z + NZ - 1) % NZ, t)
    after = ((g + 1) % 32, t)
    before = ((g + 31) % 32, t)
    far = ((1 - h) * NZ + z, t)
    core = (g, t + 1 - 2 * c)
    side = (g, (1 - x_lo) * 8 + y * 2 + c)

    def at_y(yy):
        return (g, x_lo * 8 + yy * 2 + c)

    load_rel = pltpu.make_async_copy(rel_hbm, rel, lsem.at[0])
    load_eff = pltpu.make_async_copy(eff_hbm, xe.at[pl.ds(8, TB)], lsem.at[1])
    load_coefs = [
        pltpu.make_async_copy(src, dst, lsem.at[2 + i])
        for i, (src, dst) in enumerate(
            ((one_hbm, phi_one), (two_hbm, phi_two), (scale_hbm, scale))
        )
    ]
    load_eff.start()
    for load in load_coefs:
        load.start()
    load_rel.start()

    barrier = pltpu.get_barrier_semaphore()
    peers = [up, down, after, before, far, core, side] + [
        at_y((y + d) % 4) for d in (1, 2, 3)
    ]
    for peer in peers:
        pl.semaphore_signal(barrier, inc=1, device_id=peer, device_id_type=MESH)

    for load in load_coefs:
        load.wait()
    first = g * TB
    for i in range(TB + 2):
        where = jnp.minimum(first + i, 1023)
        inside = first + i < 1024
        for row, coef in enumerate((phi_one, phi_two, scale)):
            value = jnp.where(inside, coef[where], 0.0)
            cf[row, pl.ds(8 + i, 1), :] = jnp.full((1, 128), value, jnp.float32)

    load_eff.wait()
    for k in range(FULL + 1):
        width = 128 if k < FULL else REST
        lanes = pl.ds(128 * k, width)
        for r in range(2):
            hsend[0, pl.ds(16 * r + k, 1), pl.ds(0, width)] = xe[pl.ds(38 + r, 1), lanes]
            hsend[1, pl.ds(16 * r + k, 1), pl.ds(0, width)] = xe[pl.ds(8 + r, 1), lanes]

    pl.semaphore_wait(barrier, len(peers))

    def halo(i, to):
        return pltpu.make_async_remote_copy(
            src_ref=hsend.at[i], dst_ref=hrecv.at[i], send_sem=hss.at[i],
            recv_sem=hrs.at[i], device_id=to, device_id_type=MESH,
        )

    halo(0, after).start()
    halo(1, before).start()

    def zcopy(stream, step, piece, zp):
        col = 0 if piece < 3 else 1
        rows = pl.ds(*CUTS[min(piece, 2)])
        place = gx.at[col, zp, rows]
        return pltpu.make_async_remote_copy(
            src_ref=place, dst_ref=place, send_sem=zss.at[stream, step, piece],
            recv_sem=zrs.at[stream, step, piece],
            device_id=up if stream == 0 else down, device_id_type=MESH,
        )

    def xcopy(zp, piece):
        rows = pl.ds(*CUTS[piece])
        return pltpu.make_async_remote_copy(
            src_ref=gx.at[0, zp, rows], dst_ref=gx.at[1, zp, rows],
            send_sem=xss.at[zp, piece], recv_sem=xrs.at[zp, piece],
            device_id=far, device_id_type=MESH,
        )

    def coef(i, start, rows, width):
        return cf[i, pl.ds(start, rows), pl.ds(0, width)]

    def weigh(start, rows, lanes, width):
        innov = (
            xe[pl.ds(start, rows), lanes]
            - coef(0, start, rows, width) * xe[pl.ds(start - 1, rows), lanes]
            - coef(1, start, rows, width) * xe[pl.ds(start - 2, rows), lanes]
        )
        wb[pl.ds(start, rows), lanes] = coef(2, start, rows, width) * innov

    def lag(start, rows, lanes, width):
        return (
            wb[pl.ds(start, rows), lanes]
            - coef(0, start + 1, rows, width) * wb[pl.ds(start + 1, rows), lanes]
            - coef(1, start + 2, rows, width) * wb[pl.ds(start + 2, rows), lanes]
        )

    for k in range(FULL + 1):
        width = 128 if k < FULL else REST
        lanes = pl.ds(128 * k, width)
        weigh(8, TB, lanes, width)
        mid = lag(16, 16, lanes, width)
        if k < FULL:
            gx[0, z, pl.ds(16 * k, 16), :] = mid
        else:
            gx[0, z, pl.ds(16 * k, 8), :] = jnp.concatenate([mid[:8], mid[8:]], axis=1)

    xcopy(z, 0).start()
    zcopy(0, 1, 0, z).start()
    zcopy(1, 1, 0, z).start()

    halo(0, after).wait_recv()
    halo(1, before).wait_recv()
    for k in range(FULL + 1):
        width = 128 if k < FULL else REST
        lanes = pl.ds(128 * k, width)
        for r in range(2):
            old = hrecv[0, pl.ds(16 * r + k, 1), pl.ds(0, width)]
            new = hrecv[1, pl.ds(16 * r + k, 1), pl.ds(0, width)]
            xe[pl.ds(6 + r, 1), lanes] = jnp.where(g > 0, old, 0.0)
            xe[pl.ds(40 + r, 1), lanes] = jnp.where(g < 31, new, 0.0)
    for k in range(FULL + 1):
        width = 128 if k < FULL else REST
        lanes = pl.ds(128 * k, width)
        weigh(8, 8, lanes, width)
        weigh(40, 2, lanes, width)
        head = lag(8, 8, lanes, width)
        tail = lag(32, 8, lanes, width)
        if k < FULL:
            gx[0, z, pl.ds(HALF + 16 * k, 8), :] = head
            gx[0, z, pl.ds(HALF + 16 * k + 8, 8), :] = tail
        else:
            gx[0, z, pl.ds(HALF + 16 * k, 8), :] = jnp.concatenate([head, tail], axis=1)

    xcopy(z, 2).start()
    xcopy(z, 1).start()
    for piece in (1, 2):
        zcopy(0, 1, piece, z).start()
        zcopy(1, 1, piece, z).start()
    xcopy(z, 2).wait_recv()
    zcopy(0, 1, 3, z).start()
    zcopy(1, 1, 3, z).start()
    load_rel.wait()

    def place_of(i):
        q = i // 2
        return jnp.where(i % 2 == 0, (z + q) % NZ, (z + NZ - q) % NZ)

    def core_of(zp):
        return (zp // 2) % 2

    def core_copy(zp):
        return pltpu.make_async_remote_copy(
            src_ref=part.at[zp], dst_ref=r1.at[zp], send_sem=s1s.at[zp],
            recv_sem=s1r.at[zp], device_id=core, device_id_type=MESH,
        )

    def y_copy(zp, d):
        q = (y + d) % 4
        return pltpu.make_async_remote_copy(
            src_ref=part.at[zp, :, pl.ds(pl.multiple_of(8 * q, 8), 8)],
            dst_ref=r2.at[zp, d - 1], send_sem=s2s.at[zp, d - 1],
            recv_sem=s2r.at[zp, d - 1], device_id=at_y(q), device_id_type=MESH,
        )

    mine = (h + x_lo) % 2
    quarter = pl.ds(pl.multiple_of(8 * y, 8), 8)

    def side_copy(zp):
        return pltpu.make_async_remote_copy(
            src_ref=part.at[zp, 1 - mine, quarter], dst_ref=r3.at[zp],
            send_sem=s3s.at[zp], recv_sem=s3r.at[zp],
            device_id=side, device_id_type=MESH,
        )

    def home_copy(zp, q):
        return pltpu.make_async_remote_copy(
            src_ref=part.at[zp, mine, quarter], dst_ref=done.at[zp % 2, q],
            send_sem=s4s.at[zp], recv_sem=s4r.at[zp % 2, q],
            device_id=at_y(zp // 4), device_id_type=MESH,
        )

    def split(block, at, lanes):
        high = block.astype(jnp.bfloat16)
        low = (block - high.astype(jnp.float32)).astype(jnp.bfloat16)
        lhs[pl.ds(at, 16), lanes] = high
        lhs[pl.ds(64 + at, 16), lanes] = low

    def multiply(zp):
        for col in range(2):
            for half in range(2):
                at = col * TB + half * 16
                base = half * HALF
                for k in range(FULL):
                    split(gx[col, zp, pl.ds(base + 16 * k, 16), :], at, pl.ds(128 * k, 128))
                rest = gx[col, zp, pl.ds(base + 16 * FULL, 8), :]
                rest = jnp.concatenate([rest[:, :REST], rest[:, REST:]], axis=0)
                split(rest, at, pl.ds(128 * FULL, REST))
        both = lax.dot_general(
            lhs[...], rel[...], (((1,), (1,)), ((), ())),
            preferred_element_type=jnp.float32,
        )
        total = both[:64] + both[64:]
        part[zp, 0] = total[:TB]
        part[zp, 1] = total[TB:]

    def body(i, carry):
        s = (i + 1) // 2
        zu, zd = (z + NZ - s) % NZ, (z + s) % NZ

        @pl.when((i % 2 == 1) & (i <= 16))
        def _():
            for piece in (0, 1):
                zcopy(0, s, piece, zu).wait_recv()

                @pl.when(s < 8)
                def _():
                    zcopy(0, s + 1, piece, zu).start()

                xcopy(zu, piece).start()

                @pl.when(s < 8)
                def _():
                    zcopy(1, s, piece, zd).wait_recv()

                    @pl.when(s < 7)
                    def _():
                        zcopy(1, s + 1, piece, zd).start()

                    xcopy(zd, piece).start()

        @pl.when((i % 2 == 0) & (i <= 16))
        def _():
            for piece in (2, 3):
                zcopy(1, s, piece, zd).wait_recv()

                @pl.when(s < 8)
                def _():
                    zcopy(1, s + 1, piece, zd).start()
                    zcopy(0, s, piece, zu).wait_recv()

                    @pl.when(s < 7)
                    def _():
                        zcopy(0, s + 1, piece, zu).start()

        @pl.when((i > LAG_X) & (i <= 16 + LAG_X))
        def _():
            zp = place_of(i - LAG_X)
            xcopy(zp, 0).wait_recv()
            xcopy(zp, 1).wait_recv()
            multiply(zp)

            @pl.when(core_of(zp) != c)
            def _():
                core_copy(zp).start()

        @pl.when((i > LAG_CORE) & (i <= 16 + LAG_CORE))
        def _():
            zp = place_of(i - LAG_CORE)

            @pl.when(core_of(zp) == c)
            def _():
                core_copy(zp).wait_recv()
                part[zp] = part[zp] + r1[zp]
                for d in (1, 2, 3):
                    y_copy(zp, d).start()

        @pl.when((i > LAG_Y) & (i <= 16 + LAG_Y))
        def _():
            zp = place_of(i - LAG_Y)

            @pl.when(core_of(zp) == c)
            def _():
                for d in (1, 2, 3):
                    y_copy(zp, d).wait_recv()
                both = r2[zp, 0] + (r2[zp, 1] + r2[zp, 2])
                part[zp, :, quarter] = part[zp, :, quarter] + both
                side_copy(zp).start()

        @pl.when(i > LAG_SIDE)
        def _():
            zp = place_of(i - LAG_SIDE)

            @pl.when(core_of(zp) == c)
            def _():
                side_copy(zp).wait_recv()
                total = part[zp, mine, quarter] + r3[zp]
                part[zp, mine, quarter] = total

                @pl.when(zp // 4 == y)
                def _():
                    done[zp % 2, y] = total

                @pl.when(zp // 4 != y)
                def _():
                    home_copy(zp, y).start()

        return carry

    lax.fori_loop(1, 17 + LAG_SIDE, body, 0)

    for d in (1, 2, 3):
        for b in range(2):
            home_copy(4 * y + 2 * c + b, (y + d) % 4).wait_recv()
    for b in range(2):
        for q, row in enumerate((8, 16, 0, 24)):
            out_ref[pl.ds(b * TB + row, 8), :] = done[b, q]

    halo(0, after).wait_send()
    halo(1, before).wait_send()

    def drain(s, carry):
        for stream in range(2):
            for piece in range(4):

                @pl.when((s < 8) | ((piece < 2) == (stream == 0)))
                def _():
                    zcopy(stream, s, piece, z).wait_send()

        return carry

    lax.fori_loop(1, 9, drain, 0)

    def drain_z(zp, carry):
        xcopy(zp, 0).wait_send()
        xcopy(zp, 1).wait_send()

        @pl.when(core_of(zp) != c)
        def _():
            core_copy(zp).wait_send()

        @pl.when(core_of(zp) == c)
        def _():
            for d in (1, 2, 3):
                y_copy(zp, d).wait_send()
            side_copy(zp).wait_send()

            @pl.when(zp // 4 != y)
            def _():
                home_copy(zp, y).wait_send()

        return carry

    lax.fori_loop(0, NZ, drain_z, 0)
    xcopy(z, 2).wait_send()


def on_device(relation, effects, phi_one, phi_two, innov_scale):
    dma = pltpu.SemaphoreType.DMA
    f32 = jnp.float32
    applied = pl.pallas_call(
        kernel,
        out_shape=jax.ShapeDtypeStruct((2 * TB, ANI), f32),
        in_specs=[pl.BlockSpec(memory_space=pl.ANY)] * 5,
        out_specs=pl.BlockSpec(memory_space=pltpu.VMEM),
        scratch_shapes=[
            pltpu.VMEM((ANI, COLS), jnp.bfloat16),
            pltpu.VMEM((48, COLS), f32),
            pltpu.VMEM((48, COLS), f32),
            pltpu.VMEM((3, 48, 128), f32),
            pltpu.VMEM((2, 32, 128), f32),
            pltpu.VMEM((2, 32, 128), f32),
            pltpu.VMEM((2, NZ, 2 * HALF, 128), f32),
            pltpu.VMEM((128, COLS), jnp.bfloat16),
            pltpu.VMEM((NZ, 2, TB, ANI), f32),
            pltpu.VMEM((NZ, 2, TB, ANI), f32),
            pltpu.VMEM((NZ, 3, 2, 8, ANI), f32),
            pltpu.VMEM((NZ, 8, ANI), f32),
            pltpu.VMEM((2, 4, 8, ANI), f32),
            pltpu.SMEM((1024,), f32),
            pltpu.SMEM((1024,), f32),
            pltpu.SMEM((1024,), f32),
            dma((5,)), dma((2,)), dma((2,)),
            dma((2, 9, 4)), dma((2, 9, 4)), dma((NZ, 3)), dma((NZ, 3)),
            dma((NZ,)), dma((NZ,)), dma((NZ, 3)), dma((NZ, 3)), dma((NZ,)), dma((NZ,)),
            dma((NZ,)), dma((2, 4)),
        ],
        compiler_params=pltpu.CompilerParams(
            collective_id=0, has_side_effects=True, vmem_limit_bytes=40 << 20
        ),
    )(*(pltpu.with_memory_space_constraint(a, pltpu.HBM) for a in (relation, effects.T, phi_one, phi_two, innov_scale)))
    return applied.T


def solution(mesh):
    placed = (P("gen", "tm"), P("tm", "gen"), P(), P(), P())
    return jax.shard_map(
        on_device, mesh=mesh, in_specs=placed, out_specs=P("gen", "tm"), check_vma=False
    )
```

```python
import jax
import jax.numpy as jnp
from jax import lax
from jax.experimental import pallas as pl
from jax.experimental.pallas import tpu as pltpu
from jax.sharding import PartitionSpec as P

MESH = pl.DeviceIdType.MESH
NZ = 16
ANI = 800
COLS = 1600
TB = 32
FULL = COLS // 128
REST = COLS - 128 * FULL
HALF = 200
LAG_X, LAG_CORE, LAG_Y, LAG_SIDE = 2, 3, 6, 9
CUTS = ((0, 200), (200, 40), (240, 160))


def kernel(
    rel_hbm, eff_hbm, one_hbm, two_hbm, scale_hbm, out_ref,
    rel, rel_t, xe, wb, cf, hsend, hrecv, gx, lhs, part, r1, r2, r3, done, phi_one, phi_two, scale,
    lsem, hss, hrs, zss, zrs, xss, xrs, s1s, s1r, s2s, s2r, s3s, s3r, s4s, s4r,
):
    g = lax.axis_index("gen")
    t = lax.axis_index("tm")
    h, z = g // NZ, g % NZ
    x_lo, y, c = t // 8, (t // 2) % 4, t % 2

    up = (h * NZ + (z + 1) % NZ, t)
    down = (h * NZ + (z + NZ - 1) % NZ, t)
    after = ((g + 1) % 32, t)
    before = ((g + 31) % 32, t)
    far = ((1 - h) * NZ + z, t)
    core = (g, t + 1 - 2 * c)
    side = (g, (1 - x_lo) * 8 + y * 2 + c)

    def at_y(yy):
        return (g, x_lo * 8 + yy * 2 + c)

    load_rel = pltpu.make_async_copy(rel_hbm, rel, lsem.at[0])
    load_eff = pltpu.make_async_copy(eff_hbm, xe.at[pl.ds(8, TB)], lsem.at[1])
    load_coefs = [
        pltpu.make_async_copy(src, dst, lsem.at[2 + i])
        for i, (src, dst) in enumerate(
            ((one_hbm, phi_one), (two_hbm, phi_two), (scale_hbm, scale))
        )
    ]
    load_eff.start()
    for load in load_coefs:
        load.start()
    load_rel.start()

    barrier = pltpu.get_barrier_semaphore()
    peers = [up, down, after, before, far, core, side] + [
        at_y((y + d) % 4) for d in (1, 2, 3)
    ]
    for peer in peers:
        pl.semaphore_signal(barrier, inc=1, device_id=peer, device_id_type=MESH)

    for load in load_coefs:
        load.wait()
    first = g * TB
    for i in range(TB + 2):
        where = jnp.minimum(first + i, 1023)
        inside = first + i < 1024
        for row, coef in enumerate((phi_one, phi_two, scale)):
            value = jnp.where(inside, coef[where], 0.0)
            cf[row, pl.ds(8 + i, 1), :] = jnp.full((1, 128), value, jnp.float32)

    load_eff.wait()
    for k in range(FULL + 1):
        width = 128 if k < FULL else REST
        lanes = pl.ds(128 * k, width)
        for r in range(2):
            hsend[0, pl.ds(16 * r + k, 1), pl.ds(0, width)] = xe[pl.ds(38 + r, 1), lanes]
            hsend[1, pl.ds(16 * r + k, 1), pl.ds(0, width)] = xe[pl.ds(8 + r, 1), lanes]

    pl.semaphore_wait(barrier, len(peers))

    def halo(i, to):
        return pltpu.make_async_remote_copy(
            src_ref=hsend.at[i], dst_ref=hrecv.at[i], send_sem=hss.at[i],
            recv_sem=hrs.at[i], device_id=to, device_id_type=MESH,
        )

    halo(0, after).start()
    halo(1, before).start()

    def zcopy(stream, step, piece, zp):
        col = 0 if piece < 3 else 1
        rows = pl.ds(*CUTS[min(piece, 2)])
        place = gx.at[col, zp, rows]
        return pltpu.make_async_remote_copy(
            src_ref=place, dst_ref=place, send_sem=zss.at[stream, step, piece],
            recv_sem=zrs.at[stream, step, piece],
            device_id=up if stream == 0 else down, device_id_type=MESH,
        )

    def xcopy(zp, piece):
        rows = pl.ds(*CUTS[piece])
        return pltpu.make_async_remote_copy(
            src_ref=gx.at[0, zp, rows], dst_ref=gx.at[1, zp, rows],
            send_sem=xss.at[zp, piece], recv_sem=xrs.at[zp, piece],
            device_id=far, device_id_type=MESH,
        )

    def coef(i, start, rows, width):
        return cf[i, pl.ds(start, rows), pl.ds(0, width)]

    def weigh(start, rows, lanes, width):
        innov = (
            xe[pl.ds(start, rows), lanes]
            - coef(0, start, rows, width) * xe[pl.ds(start - 1, rows), lanes]
            - coef(1, start, rows, width) * xe[pl.ds(start - 2, rows), lanes]
        )
        wb[pl.ds(start, rows), lanes] = coef(2, start, rows, width) * innov

    def lag(start, rows, lanes, width):
        return (
            wb[pl.ds(start, rows), lanes]
            - coef(0, start + 1, rows, width) * wb[pl.ds(start + 1, rows), lanes]
            - coef(1, start + 2, rows, width) * wb[pl.ds(start + 2, rows), lanes]
        )

    for k in range(FULL + 1):
        width = 128 if k < FULL else REST
        lanes = pl.ds(128 * k, width)
        weigh(8, TB, lanes, width)
        mid = lag(16, 16, lanes, width)
        if k < FULL:
            gx[0, z, pl.ds(16 * k, 16), :] = mid
        else:
            gx[0, z, pl.ds(16 * k, 8), :] = jnp.concatenate([mid[:8], mid[8:]], axis=1)

    xcopy(z, 0).start()
    zcopy(0, 1, 0, z).start()
    zcopy(1, 1, 0, z).start()

    halo(0, after).wait_recv()
    halo(1, before).wait_recv()
    for k in range(FULL + 1):
        width = 128 if k < FULL else REST
        lanes = pl.ds(128 * k, width)
        for r in range(2):
            old = hrecv[0, pl.ds(16 * r + k, 1), pl.ds(0, width)]
            new = hrecv[1, pl.ds(16 * r + k, 1), pl.ds(0, width)]
            xe[pl.ds(6 + r, 1), lanes] = jnp.where(g > 0, old, 0.0)
            xe[pl.ds(40 + r, 1), lanes] = jnp.where(g < 31, new, 0.0)
    for k in range(FULL + 1):
        width = 128 if k < FULL else REST
        lanes = pl.ds(128 * k, width)
        weigh(8, 8, lanes, width)
        weigh(40, 2, lanes, width)
        head = lag(8, 8, lanes, width)
        tail = lag(32, 8, lanes, width)
        if k < FULL:
            gx[0, z, pl.ds(HALF + 16 * k, 8), :] = head
            gx[0, z, pl.ds(HALF + 16 * k + 8, 8), :] = tail
        else:
            gx[0, z, pl.ds(HALF + 16 * k, 8), :] = jnp.concatenate([head, tail], axis=1)

    xcopy(z, 2).start()
    xcopy(z, 1).start()
    for piece in (1, 2):
        zcopy(0, 1, piece, z).start()
        zcopy(1, 1, piece, z).start()

    def place_of(i):
        q = i // 2
        return jnp.where(i % 2 == 0, (z + q) % NZ, (z + NZ - q) % NZ)

    def core_of(zp):
        return (zp // 2) % 2

    def core_copy(zp):
        return pltpu.make_async_remote_copy(
            src_ref=part.at[zp], dst_ref=r1.at[zp], send_sem=s1s.at[zp],
            recv_sem=s1r.at[zp], device_id=core, device_id_type=MESH,
        )

    def y_copy(zp, d):
        q = (y + d) % 4
        return pltpu.make_async_remote_copy(
            src_ref=part.at[zp, :, pl.ds(pl.multiple_of(8 * q, 8), 8)],
            dst_ref=r2.at[zp, d - 1], send_sem=s2s.at[zp, d - 1],
            recv_sem=s2r.at[zp, d - 1], device_id=at_y(q), device_id_type=MESH,
        )

    mine = (h + x_lo) % 2
    quarter = pl.ds(pl.multiple_of(8 * y, 8), 8)

    def side_copy(zp):
        return pltpu.make_async_remote_copy(
            src_ref=part.at[zp, 1 - mine, quarter], dst_ref=r3.at[zp],
            send_sem=s3s.at[zp], recv_sem=s3r.at[zp],
            device_id=side, device_id_type=MESH,
        )

    def home_copy(zp, q):
        return pltpu.make_async_remote_copy(
            src_ref=part.at[zp, mine, quarter], dst_ref=done.at[zp % 2, q],
            send_sem=s4s.at[zp], recv_sem=s4r.at[zp % 2, q],
            device_id=at_y(zp // 4), device_id_type=MESH,
        )

    def split(block, at, lanes):
        high = block.astype(jnp.bfloat16)
        low = (block - high.astype(jnp.float32)).astype(jnp.bfloat16)
        lhs[pl.ds(at, 16), lanes] = high
        lhs[pl.ds(64 + at, 16), lanes] = low

    def multiply(zp):
        for col in range(2):
            for half in range(2):
                at = col * TB + half * 16
                base = half * HALF
                for k in range(FULL):
                    split(gx[col, zp, pl.ds(base + 16 * k, 16), :], at, pl.ds(128 * k, 128))
                rest = gx[col, zp, pl.ds(base + 16 * FULL, 8), :]
                rest = jnp.concatenate([rest[:, :REST], rest[:, REST:]], axis=0)
                split(rest, at, pl.ds(128 * FULL, REST))
        both = lax.dot_general(
            lhs[...], rel_t[...], (((1,), (0,)), ((), ())),
            preferred_element_type=jnp.float32,
        )
        total = both[:64] + both[64:]
        part[zp, 0] = total[:TB]
        part[zp, 1] = total[TB:]

    def body(i, carry):
        s = (i + 1) // 2
        zu, zd = (z + NZ - s) % NZ, (z + s) % NZ

        @pl.when((i % 2 == 1) & (i <= 16))
        def _():
            for piece in (0, 1):
                zcopy(0, s, piece, zu).wait_recv()

                @pl.when(s < 8)
                def _():
                    zcopy(0, s + 1, piece, zu).start()

                xcopy(zu, piece).start()

                @pl.when(s < 8)
                def _():
                    zcopy(1, s, piece, zd).wait_recv()

                    @pl.when(s < 7)
                    def _():
                        zcopy(1, s + 1, piece, zd).start()

                    xcopy(zd, piece).start()

        @pl.when((i % 2 == 0) & (i <= 16))
        def _():
            for piece in (2, 3):
                zcopy(1, s, piece, zd).wait_recv()

                @pl.when(s < 8)
                def _():
                    zcopy(1, s + 1, piece, zd).start()
                    zcopy(0, s, piece, zu).wait_recv()

                    @pl.when(s < 7)
                    def _():
                        zcopy(0, s + 1, piece, zu).start()

        @pl.when(i == 1)
        def _():
            xcopy(z, 2).wait_recv()
            zcopy(0, 1, 3, z).start()
            zcopy(1, 1, 3, z).start()

        @pl.when(i == 2)
        def _():
            load_rel.wait()
            for k in range(FULL + 1):
                lanes = pl.ds(128 * k, 128 if k < FULL else REST)
                rel_t[lanes, :] = rel[:, lanes].T

        @pl.when((i > LAG_X) & (i <= 16 + LAG_X))
        def _():
            zp = place_of(i - LAG_X)
            xcopy(zp, 0).wait_recv()
            xcopy(zp, 1).wait_recv()
            multiply(zp)

            @pl.when(core_of(zp) != c)
            def _():
                core_copy(zp).start()

        @pl.when((i > LAG_CORE) & (i <= 16 + LAG_CORE))
        def _():
            zp = place_of(i - LAG_CORE)

            @pl.when(core_of(zp) == c)
            def _():
                core_copy(zp).wait_recv()
                part[zp] = part[zp] + r1[zp]
                for d in (1, 2, 3):
                    y_copy(zp, d).start()

        @pl.when((i > LAG_Y) & (i <= 16 + LAG_Y))
        def _():
            zp = place_of(i - LAG_Y)

            @pl.when(core_of(zp) == c)
            def _():
                for d in (1, 2, 3):
                    y_copy(zp, d).wait_recv()
                both = r2[zp, 0] + (r2[zp, 1] + r2[zp, 2])
                part[zp, :, quarter] = part[zp, :, quarter] + both
                side_copy(zp).start()

        @pl.when(i > LAG_SIDE)
        def _():
            zp = place_of(i - LAG_SIDE)

            @pl.when(core_of(zp) == c)
            def _():
                side_copy(zp).wait_recv()
                total = part[zp, mine, quarter] + r3[zp]
                part[zp, mine, quarter] = total

                @pl.when(zp // 4 == y)
                def _():
                    done[zp % 2, y] = total

                @pl.when(zp // 4 != y)
                def _():
                    home_copy(zp, y).start()

        return carry

    lax.fori_loop(1, 17 + LAG_SIDE, body, 0)

    for d in (1, 2, 3):
        for b in range(2):
            home_copy(4 * y + 2 * c + b, (y + d) % 4).wait_recv()
    for b in range(2):
        for q, row in enumerate((8, 16, 0, 24)):
            out_ref[pl.ds(b * TB + row, 8), :] = done[b, q]

    halo(0, after).wait_send()
    halo(1, before).wait_send()

    def drain(s, carry):
        for stream in range(2):
            for piece in range(4):

                @pl.when((s < 8) | ((piece < 2) == (stream == 0)))
                def _():
                    zcopy(stream, s, piece, z).wait_send()

        return carry

    lax.fori_loop(1, 9, drain, 0)

    def drain_z(zp, carry):
        xcopy(zp, 0).wait_send()
        xcopy(zp, 1).wait_send()

        @pl.when(core_of(zp) != c)
        def _():
            core_copy(zp).wait_send()

        @pl.when(core_of(zp) == c)
        def _():
            for d in (1, 2, 3):
                y_copy(zp, d).wait_send()
            side_copy(zp).wait_send()

            @pl.when(zp // 4 != y)
            def _():
                home_copy(zp, y).wait_send()

        return carry

    lax.fori_loop(0, NZ, drain_z, 0)
    xcopy(z, 2).wait_send()


def on_device(relation, effects, phi_one, phi_two, innov_scale):
    dma = pltpu.SemaphoreType.DMA
    f32 = jnp.float32
    applied = pl.pallas_call(
        kernel,
        out_shape=jax.ShapeDtypeStruct((2 * TB, ANI), f32),
        in_specs=[pl.BlockSpec(memory_space=pl.ANY)] * 5,
        out_specs=pl.BlockSpec(memory_space=pltpu.VMEM),
        scratch_shapes=[
            pltpu.VMEM((ANI, COLS), jnp.bfloat16),
            pltpu.VMEM((COLS, ANI), jnp.bfloat16),
            pltpu.VMEM((48, COLS), f32),
            pltpu.VMEM((48, COLS), f32),
            pltpu.VMEM((3, 48, 128), f32),
            pltpu.VMEM((2, 32, 128), f32),
            pltpu.VMEM((2, 32, 128), f32),
            pltpu.VMEM((2, NZ, 2 * HALF, 128), f32),
            pltpu.VMEM((128, COLS), jnp.bfloat16),
            pltpu.VMEM((NZ, 2, TB, ANI), f32),
            pltpu.VMEM((NZ, 2, TB, ANI), f32),
            pltpu.VMEM((NZ, 3, 2, 8, ANI), f32),
            pltpu.VMEM((NZ, 8, ANI), f32),
            pltpu.VMEM((2, 4, 8, ANI), f32),
            pltpu.SMEM((1024,), f32),
            pltpu.SMEM((1024,), f32),
            pltpu.SMEM((1024,), f32),
            dma((5,)), dma((2,)), dma((2,)),
            dma((2, 9, 4)), dma((2, 9, 4)), dma((NZ, 3)), dma((NZ, 3)),
            dma((NZ,)), dma((NZ,)), dma((NZ, 3)), dma((NZ, 3)), dma((NZ,)), dma((NZ,)),
            dma((NZ,)), dma((2, 4)),
        ],
        compiler_params=pltpu.CompilerParams(
            collective_id=0, has_side_effects=True, vmem_limit_bytes=40 << 20
        ),
    )(*(pltpu.with_memory_space_constraint(a, pltpu.HBM) for a in (relation, effects.T, phi_one, phi_two, innov_scale)))
    return applied.T


def solution(mesh):
    placed = (P("gen", "tm"), P("tm", "gen"), P(), P(), P())
    return jax.shard_map(
        on_device, mesh=mesh, in_specs=placed, out_specs=P("gen", "tm"), check_vma=False
    )
```

```python
import jax
import jax.numpy as jnp
from jax import lax
from jax.experimental import pallas as pl
from jax.experimental.pallas import tpu as pltpu
from jax.sharding import PartitionSpec as P

MESH = pl.DeviceIdType.MESH
NZ = 16
ANI = 800
COLS = 1600
TB = 32
FULL = COLS // 128
REST = COLS - 128 * FULL
HALF = 200
LAG_X, LAG_CORE, LAG_Y, LAG_SIDE = 2, 3, 6, 8
CUTS = ((0, 200), (200, 40), (240, 160))


def kernel(
    rel_hbm, eff_hbm, one_hbm, two_hbm, scale_hbm, out_ref,
    rel, rel_t, xe, wb, cf, hsend, hrecv, gx, lhs, part, r1, r2, r3, done, phi_one, phi_two, scale,
    lsem, hss, hrs, zss, zrs, xss, xrs, s1s, s1r, s2s, s2r, s3s, s3r, s4s, s4r,
):
    g = lax.axis_index("gen")
    t = lax.axis_index("tm")
    h, z = g // NZ, g % NZ
    x_lo, y, c = t // 8, (t // 2) % 4, t % 2

    up = (h * NZ + (z + 1) % NZ, t)
    down = (h * NZ + (z + NZ - 1) % NZ, t)
    after = ((g + 1) % 32, t)
    before = ((g + 31) % 32, t)
    far = ((1 - h) * NZ + z, t)
    core = (g, t + 1 - 2 * c)
    side = (g, (1 - x_lo) * 8 + y * 2 + c)

    def at_y(yy):
        return (g, x_lo * 8 + yy * 2 + c)

    load_rel = pltpu.make_async_copy(rel_hbm, rel, lsem.at[0])
    load_eff = pltpu.make_async_copy(eff_hbm, xe.at[pl.ds(8, TB)], lsem.at[1])
    load_coefs = [
        pltpu.make_async_copy(src, dst, lsem.at[2 + i])
        for i, (src, dst) in enumerate(
            ((one_hbm, phi_one), (two_hbm, phi_two), (scale_hbm, scale))
        )
    ]
    load_eff.start()
    for load in load_coefs:
        load.start()
    load_rel.start()

    barrier = pltpu.get_barrier_semaphore()
    peers = [up, down, after, before, far, core, side] + [
        at_y((y + d) % 4) for d in (1, 2, 3)
    ]
    for peer in peers:
        pl.semaphore_signal(barrier, inc=1, device_id=peer, device_id_type=MESH)

    for load in load_coefs:
        load.wait()
    first = g * TB
    for i in range(TB + 2):
        where = jnp.minimum(first + i, 1023)
        inside = first + i < 1024
        for row, coef in enumerate((phi_one, phi_two, scale)):
            value = jnp.where(inside, coef[where], 0.0)
            cf[row, pl.ds(8 + i, 1), :] = jnp.full((1, 128), value, jnp.float32)

    load_eff.wait()
    for k in range(FULL + 1):
        width = 128 if k < FULL else REST
        lanes = pl.ds(128 * k, width)
        for r in range(2):
            hsend[0, pl.ds(16 * r + k, 1), pl.ds(0, width)] = xe[pl.ds(38 + r, 1), lanes]
            hsend[1, pl.ds(16 * r + k, 1), pl.ds(0, width)] = xe[pl.ds(8 + r, 1), lanes]

    pl.semaphore_wait(barrier, len(peers))

    def halo(i, to):
        return pltpu.make_async_remote_copy(
            src_ref=hsend.at[i], dst_ref=hrecv.at[i], send_sem=hss.at[i],
            recv_sem=hrs.at[i], device_id=to, device_id_type=MESH,
        )

    halo(0, after).start()
    halo(1, before).start()

    def zcopy(stream, step, piece, zp):
        col = 0 if piece < 3 else 1
        rows = pl.ds(*CUTS[min(piece, 2)])
        place = gx.at[col, zp, rows]
        return pltpu.make_async_remote_copy(
            src_ref=place, dst_ref=place, send_sem=zss.at[stream, step, piece],
            recv_sem=zrs.at[stream, step, piece],
            device_id=up if stream == 0 else down, device_id_type=MESH,
        )

    def xcopy(zp, piece):
        rows = pl.ds(*CUTS[piece])
        return pltpu.make_async_remote_copy(
            src_ref=gx.at[0, zp, rows], dst_ref=gx.at[1, zp, rows],
            send_sem=xss.at[zp, piece], recv_sem=xrs.at[zp, piece],
            device_id=far, device_id_type=MESH,
        )

    def coef(i, start, rows, width):
        return cf[i, pl.ds(start, rows), pl.ds(0, width)]

    def weigh(start, rows, lanes, width):
        innov = (
            xe[pl.ds(start, rows), lanes]
            - coef(0, start, rows, width) * xe[pl.ds(start - 1, rows), lanes]
            - coef(1, start, rows, width) * xe[pl.ds(start - 2, rows), lanes]
        )
        wb[pl.ds(start, rows), lanes] = coef(2, start, rows, width) * innov

    def lag(start, rows, lanes, width):
        return (
            wb[pl.ds(start, rows), lanes]
            - coef(0, start + 1, rows, width) * wb[pl.ds(start + 1, rows), lanes]
            - coef(1, start + 2, rows, width) * wb[pl.ds(start + 2, rows), lanes]
        )

    for k in range(FULL + 1):
        width = 128 if k < FULL else REST
        lanes = pl.ds(128 * k, width)
        weigh(8, TB, lanes, width)
        mid = lag(16, 16, lanes, width)
        if k < FULL:
            gx[0, z, pl.ds(16 * k, 16), :] = mid
        else:
            gx[0, z, pl.ds(16 * k, 8), :] = jnp.concatenate([mid[:8], mid[8:]], axis=1)

    xcopy(z, 0).start()
    zcopy(0, 1, 0, z).start()
    zcopy(1, 1, 0, z).start()

    halo(0, after).wait_recv()
    halo(1, before).wait_recv()
    for k in range(FULL + 1):
        width = 128 if k < FULL else REST
        lanes = pl.ds(128 * k, width)
        for r in range(2):
            old = hrecv[0, pl.ds(16 * r + k, 1), pl.ds(0, width)]
            new = hrecv[1, pl.ds(16 * r + k, 1), pl.ds(0, width)]
            xe[pl.ds(6 + r, 1), lanes] = jnp.where(g > 0, old, 0.0)
            xe[pl.ds(40 + r, 1), lanes] = jnp.where(g < 31, new, 0.0)
    for k in range(FULL + 1):
        width = 128 if k < FULL else REST
        lanes = pl.ds(128 * k, width)
        weigh(8, 8, lanes, width)
        weigh(40, 2, lanes, width)
        head = lag(8, 8, lanes, width)
        tail = lag(32, 8, lanes, width)
        if k < FULL:
            gx[0, z, pl.ds(HALF + 16 * k, 8), :] = head
            gx[0, z, pl.ds(HALF + 16 * k + 8, 8), :] = tail
        else:
            gx[0, z, pl.ds(HALF + 16 * k, 8), :] = jnp.concatenate([head, tail], axis=1)

    xcopy(z, 2).start()
    xcopy(z, 1).start()
    for piece in (1, 2):
        zcopy(0, 1, piece, z).start()
        zcopy(1, 1, piece, z).start()

    def place_of(i):
        q = i // 2
        return jnp.where(i % 2 == 0, (z + q) % NZ, (z + NZ - q) % NZ)

    def core_of(zp):
        return (zp // 2) % 2

    def core_copy(zp):
        return pltpu.make_async_remote_copy(
            src_ref=part.at[zp], dst_ref=r1.at[zp], send_sem=s1s.at[zp],
            recv_sem=s1r.at[zp], device_id=core, device_id_type=MESH,
        )

    def y_copy(zp, d):
        q = (y + d) % 4
        return pltpu.make_async_remote_copy(
            src_ref=part.at[zp, :, pl.ds(pl.multiple_of(8 * q, 8), 8)],
            dst_ref=r2.at[zp, d - 1], send_sem=s2s.at[zp, d - 1],
            recv_sem=s2r.at[zp, d - 1], device_id=at_y(q), device_id_type=MESH,
        )

    mine = (h + x_lo) % 2
    quarter = pl.ds(pl.multiple_of(8 * y, 8), 8)

    def side_copy(zp):
        return pltpu.make_async_remote_copy(
            src_ref=part.at[zp, 1 - mine, quarter], dst_ref=r3.at[zp],
            send_sem=s3s.at[zp], recv_sem=s3r.at[zp],
            device_id=side, device_id_type=MESH,
        )

    def home_copy(zp, q):
        return pltpu.make_async_remote_copy(
            src_ref=part.at[zp, mine, quarter], dst_ref=done.at[zp % 2, q],
            send_sem=s4s.at[zp], recv_sem=s4r.at[zp % 2, q],
            device_id=at_y(zp // 4), device_id_type=MESH,
        )

    def split(block, at, lanes):
        high = block.astype(jnp.bfloat16)
        low = (block - high.astype(jnp.float32)).astype(jnp.bfloat16)
        lhs[pl.ds(at, 16), lanes] = high
        lhs[pl.ds(64 + at, 16), lanes] = low

    def multiply(zp):
        for col in range(2):
            for half in range(2):
                at = col * TB + half * 16
                base = half * HALF
                for k in range(FULL):
                    split(gx[col, zp, pl.ds(base + 16 * k, 16), :], at, pl.ds(128 * k, 128))
                rest = gx[col, zp, pl.ds(base + 16 * FULL, 8), :]
                rest = jnp.concatenate([rest[:, :REST], rest[:, REST:]], axis=0)
                split(rest, at, pl.ds(128 * FULL, REST))
        both = lax.dot_general(
            lhs[...], rel_t[...], (((1,), (0,)), ((), ())),
            preferred_element_type=jnp.float32,
        )
        total = both[:64] + both[64:]
        part[zp, 0] = total[:TB]
        part[zp, 1] = total[TB:]

    def body(i, carry):
        s = (i + 1) // 2
        zu, zd = (z + NZ - s) % NZ, (z + s) % NZ

        @pl.when((i % 2 == 1) & (i <= 16))
        def _():
            for piece in (0, 1):
                zcopy(0, s, piece, zu).wait_recv()

                @pl.when(s < 8)
                def _():
                    zcopy(0, s + 1, piece, zu).start()

                xcopy(zu, piece).start()

                @pl.when(s < 8)
                def _():
                    zcopy(1, s, piece, zd).wait_recv()

                    @pl.when(s < 7)
                    def _():
                        zcopy(1, s + 1, piece, zd).start()

                    xcopy(zd, piece).start()

        @pl.when((i % 2 == 0) & (i <= 16))
        def _():
            for piece in (2, 3):
                zcopy(1, s, piece, zd).wait_recv()

                @pl.when(s < 8)
                def _():
                    zcopy(1, s + 1, piece, zd).start()
                    zcopy(0, s, piece, zu).wait_recv()

                    @pl.when(s < 7)
                    def _():
                        zcopy(0, s + 1, piece, zu).start()

        @pl.when(i == 1)
        def _():
            xcopy(z, 2).wait_recv()
            zcopy(0, 1, 3, z).start()
            zcopy(1, 1, 3, z).start()

        @pl.when(i == 2)
        def _():
            load_rel.wait()
            for k in range(FULL + 1):
                lanes = pl.ds(128 * k, 128 if k < FULL else REST)
                rel_t[lanes, :] = rel[:, lanes].T

        @pl.when((i > LAG_X) & (i <= 16 + LAG_X))
        def _():
            zp = place_of(i - LAG_X)
            xcopy(zp, 0).wait_recv()
            xcopy(zp, 1).wait_recv()
            multiply(zp)

            @pl.when(core_of(zp) != c)
            def _():
                core_copy(zp).start()

        @pl.when((i > LAG_CORE) & (i <= 16 + LAG_CORE))
        def _():
            zp = place_of(i - LAG_CORE)

            @pl.when(core_of(zp) == c)
            def _():
                core_copy(zp).wait_recv()
                part[zp] = part[zp] + r1[zp]
                for d in (1, 2, 3):
                    y_copy(zp, d).start()

        @pl.when((i > LAG_Y) & (i <= 16 + LAG_Y))
        def _():
            zp = place_of(i - LAG_Y)

            @pl.when(core_of(zp) == c)
            def _():
                for d in (1, 2, 3):
                    y_copy(zp, d).wait_recv()
                both = r2[zp, 0] + (r2[zp, 1] + r2[zp, 2])
                part[zp, :, quarter] = part[zp, :, quarter] + both
                side_copy(zp).start()

        @pl.when(i > LAG_SIDE)
        def _():
            zp = place_of(i - LAG_SIDE)

            @pl.when(core_of(zp) == c)
            def _():
                side_copy(zp).wait_recv()
                total = part[zp, mine, quarter] + r3[zp]
                part[zp, mine, quarter] = total

                @pl.when(zp // 4 == y)
                def _():
                    done[zp % 2, y] = total

                @pl.when(zp // 4 != y)
                def _():
                    home_copy(zp, y).start()

        return carry

    lax.fori_loop(1, 17 + LAG_SIDE, body, 0)

    for d in (1, 2, 3):
        for b in range(2):
            home_copy(4 * y + 2 * c + b, (y + d) % 4).wait_recv()
    for b in range(2):
        for q, row in enumerate((8, 16, 0, 24)):
            out_ref[pl.ds(b * TB + row, 8), :] = done[b, q]

    halo(0, after).wait_send()
    halo(1, before).wait_send()

    def drain(s, carry):
        for stream in range(2):
            for piece in range(4):

                @pl.when((s < 8) | ((piece < 2) == (stream == 0)))
                def _():
                    zcopy(stream, s, piece, z).wait_send()

        return carry

    lax.fori_loop(1, 9, drain, 0)

    def drain_z(zp, carry):
        xcopy(zp, 0).wait_send()
        xcopy(zp, 1).wait_send()

        @pl.when(core_of(zp) != c)
        def _():
            core_copy(zp).wait_send()

        @pl.when(core_of(zp) == c)
        def _():
            for d in (1, 2, 3):
                y_copy(zp, d).wait_send()
            side_copy(zp).wait_send()

            @pl.when(zp // 4 != y)
            def _():
                home_copy(zp, y).wait_send()

        return carry

    lax.fori_loop(0, NZ, drain_z, 0)
    xcopy(z, 2).wait_send()


def on_device(relation, effects, phi_one, phi_two, innov_scale):
    dma = pltpu.SemaphoreType.DMA
    f32 = jnp.float32
    applied = pl.pallas_call(
        kernel,
        out_shape=jax.ShapeDtypeStruct((2 * TB, ANI), f32),
        in_specs=[pl.BlockSpec(memory_space=pl.ANY)] * 5,
        out_specs=pl.BlockSpec(memory_space=pltpu.VMEM),
        scratch_shapes=[
            pltpu.VMEM((ANI, COLS), jnp.bfloat16),
            pltpu.VMEM((COLS, ANI), jnp.bfloat16),
            pltpu.VMEM((48, COLS), f32),
            pltpu.VMEM((48, COLS), f32),
            pltpu.VMEM((3, 48, 128), f32),
            pltpu.VMEM((2, 32, 128), f32),
            pltpu.VMEM((2, 32, 128), f32),
            pltpu.VMEM((2, NZ, 2 * HALF, 128), f32),
            pltpu.VMEM((128, COLS), jnp.bfloat16),
            pltpu.VMEM((NZ, 2, TB, ANI), f32),
            pltpu.VMEM((NZ, 2, TB, ANI), f32),
            pltpu.VMEM((NZ, 3, 2, 8, ANI), f32),
            pltpu.VMEM((NZ, 8, ANI), f32),
            pltpu.VMEM((2, 4, 8, ANI), f32),
            pltpu.SMEM((1024,), f32),
            pltpu.SMEM((1024,), f32),
            pltpu.SMEM((1024,), f32),
            dma((5,)), dma((2,)), dma((2,)),
            dma((2, 9, 4)), dma((2, 9, 4)), dma((NZ, 3)), dma((NZ, 3)),
            dma((NZ,)), dma((NZ,)), dma((NZ, 3)), dma((NZ, 3)), dma((NZ,)), dma((NZ,)),
            dma((NZ,)), dma((2, 4)),
        ],
        compiler_params=pltpu.CompilerParams(
            collective_id=0, has_side_effects=True, vmem_limit_bytes=40 << 20
        ),
    )(*(pltpu.with_memory_space_constraint(a, pltpu.HBM) for a in (relation, effects.T, phi_one, phi_two, innov_scale)))
    return applied.T


def solution(mesh):
    placed = (P("gen", "tm"), P("tm", "gen"), P(), P(), P())
    return jax.shard_map(
        on_device, mesh=mesh, in_specs=placed, out_specs=P("gen", "tm"), check_vma=False
    )
```

```python
import jax
import jax.numpy as jnp
from jax import lax
from jax.experimental import pallas as pl
from jax.experimental.pallas import tpu as pltpu
from jax.sharding import PartitionSpec as P

MESH = pl.DeviceIdType.MESH
NZ = 16
ANI = 800
COLS = 1600
TB = 32
FULL = COLS // 128
REST = COLS - 128 * FULL
HALF = 200
LAG_X, LAG_CORE, LAG_Y, LAG_SIDE = 2, 3, 6, 8
CUTS = ((0, 200), (200, 48), (248, 152))


def kernel(
    rel_hbm, eff_hbm, one_hbm, two_hbm, scale_hbm, out_ref,
    rel, rel_t, xe, wb, cf, hsend, hrecv, gx, lhs, part, r1, r2, r3, done, phi_one, phi_two, scale,
    lsem, hss, hrs, zss, zrs, xss, xrs, s1s, s1r, s2s, s2r, s3s, s3r, s4s, s4r,
):
    g = lax.axis_index("gen")
    t = lax.axis_index("tm")
    h, z = g // NZ, g % NZ
    x_lo, y, c = t // 8, (t // 2) % 4, t % 2

    up = (h * NZ + (z + 1) % NZ, t)
    down = (h * NZ + (z + NZ - 1) % NZ, t)
    after = ((g + 1) % 32, t)
    before = ((g + 31) % 32, t)
    far = ((1 - h) * NZ + z, t)
    core = (g, t + 1 - 2 * c)
    side = (g, (1 - x_lo) * 8 + y * 2 + c)

    def at_y(yy):
        return (g, x_lo * 8 + yy * 2 + c)

    load_rel = pltpu.make_async_copy(rel_hbm, rel, lsem.at[0])
    load_eff = pltpu.make_async_copy(eff_hbm, xe.at[pl.ds(8, TB)], lsem.at[1])
    load_coefs = [
        pltpu.make_async_copy(src, dst, lsem.at[2 + i])
        for i, (src, dst) in enumerate(
            ((one_hbm, phi_one), (two_hbm, phi_two), (scale_hbm, scale))
        )
    ]
    load_eff.start()
    for load in load_coefs:
        load.start()
    load_rel.start()

    barrier = pltpu.get_barrier_semaphore()
    peers = [up, down, after, before, far, core, side] + [
        at_y((y + d) % 4) for d in (1, 2, 3)
    ]
    for peer in peers:
        pl.semaphore_signal(barrier, inc=1, device_id=peer, device_id_type=MESH)

    for load in load_coefs:
        load.wait()
    first = g * TB
    for i in range(TB + 2):
        where = jnp.minimum(first + i, 1023)
        inside = first + i < 1024
        for row, coef in enumerate((phi_one, phi_two, scale)):
            value = jnp.where(inside, coef[where], 0.0)
            cf[row, pl.ds(8 + i, 1), :] = jnp.full((1, 128), value, jnp.float32)

    load_eff.wait()
    for k in range(FULL + 1):
        width = 128 if k < FULL else REST
        lanes = pl.ds(128 * k, width)
        for r in range(2):
            hsend[0, pl.ds(16 * r + k, 1), pl.ds(0, width)] = xe[pl.ds(38 + r, 1), lanes]
            hsend[1, pl.ds(16 * r + k, 1), pl.ds(0, width)] = xe[pl.ds(8 + r, 1), lanes]

    pl.semaphore_wait(barrier, len(peers))

    def halo(i, to):
        return pltpu.make_async_remote_copy(
            src_ref=hsend.at[i], dst_ref=hrecv.at[i], send_sem=hss.at[i],
            recv_sem=hrs.at[i], device_id=to, device_id_type=MESH,
        )

    halo(0, after).start()
    halo(1, before).start()

    def zcopy(stream, step, piece, zp):
        col = 0 if piece < 3 else 1
        rows = pl.ds(*CUTS[min(piece, 2)])
        place = gx.at[col, zp, rows]
        return pltpu.make_async_remote_copy(
            src_ref=place, dst_ref=place, send_sem=zss.at[stream, step, piece],
            recv_sem=zrs.at[stream, step, piece],
            device_id=up if stream == 0 else down, device_id_type=MESH,
        )

    def xcopy(zp, piece):
        rows = pl.ds(*CUTS[piece])
        return pltpu.make_async_remote_copy(
            src_ref=gx.at[0, zp, rows], dst_ref=gx.at[1, zp, rows],
            send_sem=xss.at[zp, piece], recv_sem=xrs.at[zp, piece],
            device_id=far, device_id_type=MESH,
        )

    def coef(i, start, rows, width):
        return cf[i, pl.ds(start, rows), pl.ds(0, width)]

    def weigh(start, rows, lanes, width):
        innov = (
            xe[pl.ds(start, rows), lanes]
            - coef(0, start, rows, width) * xe[pl.ds(start - 1, rows), lanes]
            - coef(1, start, rows, width) * xe[pl.ds(start - 2, rows), lanes]
        )
        wb[pl.ds(start, rows), lanes] = coef(2, start, rows, width) * innov

    def lag(start, rows, lanes, width):
        return (
            wb[pl.ds(start, rows), lanes]
            - coef(0, start + 1, rows, width) * wb[pl.ds(start + 1, rows), lanes]
            - coef(1, start + 2, rows, width) * wb[pl.ds(start + 2, rows), lanes]
        )

    for k in range(FULL + 1):
        width = 128 if k < FULL else REST
        lanes = pl.ds(128 * k, width)
        weigh(8, TB, lanes, width)
        mid = lag(16, 16, lanes, width)
        if k < FULL:
            gx[0, z, pl.ds(16 * k, 16), :] = mid
        else:
            gx[0, z, pl.ds(16 * k, 8), :] = jnp.concatenate([mid[:8], mid[8:]], axis=1)

    xcopy(z, 0).start()
    zcopy(0, 1, 0, z).start()
    zcopy(1, 1, 0, z).start()

    halo(0, after).wait_recv()
    halo(1, before).wait_recv()
    for k in range(FULL + 1):
        width = 128 if k < FULL else REST
        lanes = pl.ds(128 * k, width)
        for r in range(2):
            old = hrecv[0, pl.ds(16 * r + k, 1), pl.ds(0, width)]
            new = hrecv[1, pl.ds(16 * r + k, 1), pl.ds(0, width)]
            xe[pl.ds(6 + r, 1), lanes] = jnp.where(g > 0, old, 0.0)
            xe[pl.ds(40 + r, 1), lanes] = jnp.where(g < 31, new, 0.0)
    for k in range(FULL + 1):
        width = 128 if k < FULL else REST
        lanes = pl.ds(128 * k, width)
        weigh(8, 8, lanes, width)
        weigh(40, 2, lanes, width)
        head = lag(8, 8, lanes, width)
        tail = lag(32, 8, lanes, width)
        if k < FULL:
            gx[0, z, pl.ds(HALF + 16 * k, 8), :] = head
            gx[0, z, pl.ds(HALF + 16 * k + 8, 8), :] = tail
        else:
            gx[0, z, pl.ds(HALF + 16 * k, 8), :] = jnp.concatenate([head, tail], axis=1)

    xcopy(z, 2).start()
    xcopy(z, 1).start()
    for piece in (1, 2):
        zcopy(0, 1, piece, z).start()
        zcopy(1, 1, piece, z).start()

    def place_of(i):
        q = i // 2
        return jnp.where(i % 2 == 0, (z + q) % NZ, (z + NZ - q) % NZ)

    def core_of(zp):
        return (zp // 2) % 2

    def core_copy(zp):
        return pltpu.make_async_remote_copy(
            src_ref=part.at[zp], dst_ref=r1.at[zp], send_sem=s1s.at[zp],
            recv_sem=s1r.at[zp], device_id=core, device_id_type=MESH,
        )

    def y_copy(zp, d):
        q = (y + d) % 4
        return pltpu.make_async_remote_copy(
            src_ref=part.at[zp, :, pl.ds(pl.multiple_of(8 * q, 8), 8)],
            dst_ref=r2.at[zp, d - 1], send_sem=s2s.at[zp, d - 1],
            recv_sem=s2r.at[zp, d - 1], device_id=at_y(q), device_id_type=MESH,
        )

    mine = (h + x_lo) % 2
    quarter = pl.ds(pl.multiple_of(8 * y, 8), 8)

    def side_copy(zp):
        return pltpu.make_async_remote_copy(
            src_ref=part.at[zp, 1 - mine, quarter], dst_ref=r3.at[zp],
            send_sem=s3s.at[zp], recv_sem=s3r.at[zp],
            device_id=side, device_id_type=MESH,
        )

    def home_copy(zp, q):
        return pltpu.make_async_remote_copy(
            src_ref=part.at[zp, mine, quarter], dst_ref=done.at[zp % 2, q],
            send_sem=s4s.at[zp], recv_sem=s4r.at[zp % 2, q],
            device_id=at_y(zp // 4), device_id_type=MESH,
        )

    def split(block, at, lanes):
        high = block.astype(jnp.bfloat16)
        low = (block - high.astype(jnp.float32)).astype(jnp.bfloat16)
        lhs[pl.ds(at, 16), lanes] = high
        lhs[pl.ds(64 + at, 16), lanes] = low

    def multiply(zp):
        for col in range(2):
            for half in range(2):
                at = col * TB + half * 16
                base = half * HALF
                for k in range(FULL):
                    split(gx[col, zp, pl.ds(base + 16 * k, 16), :], at, pl.ds(128 * k, 128))
                rest = gx[col, zp, pl.ds(base + 16 * FULL, 8), :]
                rest = jnp.concatenate([rest[:, :REST], rest[:, REST:]], axis=0)
                split(rest, at, pl.ds(128 * FULL, REST))
        both = lax.dot_general(
            lhs[...], rel_t[...], (((1,), (0,)), ((), ())),
            preferred_element_type=jnp.float32,
        )
        total = both[:64] + both[64:]
        part[zp, 0] = total[:TB]
        part[zp, 1] = total[TB:]

    def body(i, carry):
        s = (i + 1) // 2
        zu, zd = (z + NZ - s) % NZ, (z + s) % NZ

        @pl.when((i % 2 == 1) & (i <= 16))
        def _():
            for piece in (0, 1):
                zcopy(0, s, piece, zu).wait_recv()

                @pl.when(s < 8)
                def _():
                    zcopy(0, s + 1, piece, zu).start()

                xcopy(zu, piece).start()

                @pl.when(s < 8)
                def _():
                    zcopy(1, s, piece, zd).wait_recv()

                    @pl.when(s < 7)
                    def _():
                        zcopy(1, s + 1, piece, zd).start()

                    xcopy(zd, piece).start()

        @pl.when((i % 2 == 0) & (i <= 16))
        def _():
            for piece in (2, 3):
                zcopy(1, s, piece, zd).wait_recv()

                @pl.when(s < 8)
                def _():
                    zcopy(1, s + 1, piece, zd).start()
                    zcopy(0, s, piece, zu).wait_recv()

                    @pl.when(s < 7)
                    def _():
                        zcopy(0, s + 1, piece, zu).start()

        @pl.when(i == 1)
        def _():
            xcopy(z, 2).wait_recv()
            zcopy(0, 1, 3, z).start()
            zcopy(1, 1, 3, z).start()

        @pl.when(i == 2)
        def _():
            load_rel.wait()
            for k in range(FULL + 1):
                lanes = pl.ds(128 * k, 128 if k < FULL else REST)
                rel_t[lanes, :] = rel[:, lanes].T

        @pl.when((i > LAG_X) & (i <= 16 + LAG_X))
        def _():
            zp = place_of(i - LAG_X)
            xcopy(zp, 0).wait_recv()
            xcopy(zp, 1).wait_recv()
            multiply(zp)

            @pl.when(core_of(zp) != c)
            def _():
                core_copy(zp).start()

        @pl.when((i > LAG_CORE) & (i <= 16 + LAG_CORE))
        def _():
            zp = place_of(i - LAG_CORE)

            @pl.when(core_of(zp) == c)
            def _():
                core_copy(zp).wait_recv()
                part[zp] = part[zp] + r1[zp]
                for d in (1, 2, 3):
                    y_copy(zp, d).start()

        @pl.when((i > LAG_Y) & (i <= 16 + LAG_Y))
        def _():
            zp = place_of(i - LAG_Y)

            @pl.when(core_of(zp) == c)
            def _():
                for d in (1, 2, 3):
                    y_copy(zp, d).wait_recv()
                both = r2[zp, 0] + (r2[zp, 1] + r2[zp, 2])
                part[zp, :, quarter] = part[zp, :, quarter] + both
                side_copy(zp).start()

        @pl.when(i > LAG_SIDE)
        def _():
            zp = place_of(i - LAG_SIDE)

            @pl.when(core_of(zp) == c)
            def _():
                side_copy(zp).wait_recv()
                total = part[zp, mine, quarter] + r3[zp]
                part[zp, mine, quarter] = total

                @pl.when(zp // 4 == y)
                def _():
                    done[zp % 2, y] = total

                @pl.when(zp // 4 != y)
                def _():
                    home_copy(zp, y).start()

        return carry

    lax.fori_loop(1, 17 + LAG_SIDE, body, 0)

    for d in (1, 2, 3):
        for b in range(2):
            home_copy(4 * y + 2 * c + b, (y + d) % 4).wait_recv()
    for b in range(2):
        for q, row in enumerate((8, 16, 0, 24)):
            out_ref[pl.ds(b * TB + row, 8), :] = done[b, q]

    halo(0, after).wait_send()
    halo(1, before).wait_send()

    def drain(s, carry):
        for stream in range(2):
            for piece in range(4):

                @pl.when((s < 8) | ((piece < 2) == (stream == 0)))
                def _():
                    zcopy(stream, s, piece, z).wait_send()

        return carry

    lax.fori_loop(1, 9, drain, 0)

    def drain_z(zp, carry):
        xcopy(zp, 0).wait_send()
        xcopy(zp, 1).wait_send()

        @pl.when(core_of(zp) != c)
        def _():
            core_copy(zp).wait_send()

        @pl.when(core_of(zp) == c)
        def _():
            for d in (1, 2, 3):
                y_copy(zp, d).wait_send()
            side_copy(zp).wait_send()

            @pl.when(zp // 4 != y)
            def _():
                home_copy(zp, y).wait_send()

        return carry

    lax.fori_loop(0, NZ, drain_z, 0)
    xcopy(z, 2).wait_send()


def on_device(relation, effects, phi_one, phi_two, innov_scale):
    dma = pltpu.SemaphoreType.DMA
    f32 = jnp.float32
    applied = pl.pallas_call(
        kernel,
        out_shape=jax.ShapeDtypeStruct((2 * TB, ANI), f32),
        in_specs=[pl.BlockSpec(memory_space=pl.ANY)] * 5,
        out_specs=pl.BlockSpec(memory_space=pltpu.VMEM),
        scratch_shapes=[
            pltpu.VMEM((ANI, COLS), jnp.bfloat16),
            pltpu.VMEM((COLS, ANI), jnp.bfloat16),
            pltpu.VMEM((48, COLS), f32),
            pltpu.VMEM((48, COLS), f32),
            pltpu.VMEM((3, 48, 128), f32),
            pltpu.VMEM((2, 32, 128), f32),
            pltpu.VMEM((2, 32, 128), f32),
            pltpu.VMEM((2, NZ, 2 * HALF, 128), f32),
            pltpu.VMEM((128, COLS), jnp.bfloat16),
            pltpu.VMEM((NZ, 2, TB, ANI), f32),
            pltpu.VMEM((NZ, 2, TB, ANI), f32),
            pltpu.VMEM((NZ, 3, 2, 8, ANI), f32),
            pltpu.VMEM((NZ, 8, ANI), f32),
            pltpu.VMEM((2, 4, 8, ANI), f32),
            pltpu.SMEM((1024,), f32),
            pltpu.SMEM((1024,), f32),
            pltpu.SMEM((1024,), f32),
            dma((5,)), dma((2,)), dma((2,)),
            dma((2, 9, 4)), dma((2, 9, 4)), dma((NZ, 3)), dma((NZ, 3)),
            dma((NZ,)), dma((NZ,)), dma((NZ, 3)), dma((NZ, 3)), dma((NZ,)), dma((NZ,)),
            dma((NZ,)), dma((2, 4)),
        ],
        compiler_params=pltpu.CompilerParams(
            collective_id=0, has_side_effects=True, vmem_limit_bytes=40 << 20
        ),
    )(*(pltpu.with_memory_space_constraint(a, pltpu.HBM) for a in (relation, effects.T, phi_one, phi_two, innov_scale)))
    return applied.T


def solution(mesh):
    placed = (P("gen", "tm"), P("tm", "gen"), P(), P(), P())
    return jax.shard_map(
        on_device, mesh=mesh, in_specs=placed, out_specs=P("gen", "tm"), check_vma=False
    )
```
